32 devices in a mesh: scene: 2 (over x), tile: 8 (over z, y), chan: 2 (over core).
Axes of the slice: x: 2, y: 2, z: 4, core: 2. Of those that a mesh axis runs over, the one named last changes fastest.
Arguments:
- raw_echoes: bfloat16 [256, 12, 2, 2048], P(('scene', 'tile'), 'chan'), parts along dimension 0, may hold values from -6 to 6
- range_taps: bfloat16 [12, 2, 512], replicated, may hold values from -0.1875 to 0.1875
- beam_weights: bfloat16 [12, 2, 2048], replicated, may hold values from -1.1953125 to 1.1953125
- channel_order: int32 [12], replicated, may hold values from 0 to 11, each once
- group_cells: int32 [8], replicated, may hold values from 128 to 384, as said below
- tap_counts: int32 [2048], replicated, may hold values from 384 to 640, as said below
- chirp_rates: float32 [2048], replicated, may hold values from 0.5 to 2
Outputs:
- focused_image: float32 [6144, 2, 128], P(('scene', 'tile', 'chan')), parts along dimension 0
The draws below stay inside these ranges and needn't reach their ends.
There are 2 independent parts, one for each index of `scene`. The reference program is written for one: setup_inputs(seed, part) draws one part's arguments, and reference() takes and returns one part's arrays. A program takes and returns all parts, laid end to end along the dimension named above; an argument that names none is the same for every part. Nothing has to cross between parts.
Inputs may be any that keep to these rules, and one draw needn't show every extreme that they name: `channel_order`: A permutation of the channels. `group_cells`: the counts sum to 2048; devices 2i and 2i + 1 of tile together own 2 * 256 cells; at least one device owns exactly 384. `tap_counts`: the first range cell has 384 taps and the last 640; counts rise with range up to a small jitter.
All inputs are finite; a program needn't handle non-finite values.
Results may differ from the reference program's by a relative error of at most 0.0053.
Values may be sent and summed in bfloat16 or wider, within the bound.
A program may use at most 320 MiB of HBM per device.

```python
import math
import jax
import jax.numpy as jnp
from jax import lax

R = 2048
C = 12
L = 512
KMAX = 640
KMIN = 384
PUL_DEV = 16
P_SIZE = 128
CH_DEV = 6
SHARE = 256
MAXG = 384
SLOTS = 3072
N_TILE = 8
N_CHAN = 2


def draw_group_cells(key, part):
    average = R // N_TILE
    couples = N_TILE // 2
    key_spread = jax.random.fold_in(key, 11)
    key_widest = jax.random.fold_in(key, 12)
    key_orient = jax.random.fold_in(key, 13)
    spread = jax.random.randint(key_spread, (couples,), 0, average // 2 + 1)
    widest = jax.random.randint(key_widest, (), 0, couples)
    spread = jnp.where(jnp.arange(couples) == widest, average // 2, spread)
    orient = jax.random.randint(key_orient, (couples,), 0, 2) * 2 - 1
    leading_cells = average + orient * spread
    trailing_cells = average - orient * spread
    return jnp.stack([leading_cells, trailing_cells], 1).reshape(N_TILE).astype(jnp.int32)


def draw_tap_counts(key, part):
    position = jnp.arange(R, dtype=jnp.int32)
    tap_span = KMAX - KMIN
    slope_base = KMIN + tap_span * position // max(R - 1, 1)
    jitter_reach = max(tap_span // 32, 1)
    jitter = jax.random.randint(jax.random.fold_in(key, 21), (R,), -jitter_reach, jitter_reach + 1)
    interior = (position > 0) & (position < R - 1)
    jitter = jnp.where(interior, jitter, 0)
    return jnp.clip(slope_base + jitter, KMIN, KMAX).astype(jnp.int32)


def levels(own_key, shape, split, low, largest):
    def one(dim, shards_of):
        draws = jax.random.uniform(jax.random.fold_in(jax.random.fold_in(own_key, 6), dim), (shards_of,), jnp.float32, low / len(split), largest / len(split))
        return jnp.repeat(jnp.exp(draws), shape[dim] // shards_of).reshape((-1,) + (1,) * (len(shape) - dim - 1))

    gain = one(*split[0])
    for cut in split[1:]:
        gain = gain * one(*cut)
    return gain


def noise(own_key, shape, width, most, split=(), kind=jnp.bfloat16):
    drawn = jax.random.normal(own_key, shape, jnp.float32) * width
    if len(split) > 0:
        drawn = levels(own_key, shape, split, -0.22, 0.18) * drawn
    return jnp.clip(drawn, min=-most, max=most).astype(kind)


def setup_inputs(seed: int = 0, part: int = 0) -> dict:
    keys = jax.random.split(jax.random.key(seed), 8)
    part_splits = jax.random.split(jax.random.fold_in(keys[7], part), 8)
    raw_echoes = noise(part_splits[0], (P_SIZE, C, 2, R), 1.0, 6.0, ((0, 8), (1, 2)))
    range_taps = noise(keys[1], (C, 2, L), (2 * L) ** -0.5, 0.1875)
    beam_weights = noise(keys[2], (C, 2, R), 0.2, 1.1953125)
    channel_order = jax.random.permutation(keys[3], C).astype(jnp.int32)
    group_cells = draw_group_cells(jax.random.fold_in(keys[7], 71), part)
    tap_counts = draw_tap_counts(jax.random.fold_in(keys[7], 71), part)
    chirp_rates = jnp.clip(jnp.exp(jax.random.uniform(keys[6], (R,), jnp.float32, math.log(0.5), math.log(2.0))), 0.5, 2.0)
    return {"raw_echoes": raw_echoes, "range_taps": range_taps, "beam_weights": beam_weights, "channel_order": channel_order, "group_cells": group_cells, "tap_counts": tap_counts, "chirp_rates": chirp_rates}


def toeplitz_rows(coeffs, block_len, span_len):
    leading = coeffs.shape[:-1]
    filler = jnp.zeros(leading + (span_len + 1 - coeffs.shape[-1],), coeffs.dtype)
    extended = jnp.concatenate([coeffs, filler], -1)
    repeated = jnp.tile(extended, (1,) * len(leading) + (block_len,))
    return repeated[..., :block_len * span_len].reshape(leading + (block_len, span_len))

def complex_matrix(toeplitz_pair):
    real_part = toeplitz_pair[..., 0, :, :]
    imag_part = toeplitz_pair[..., 1, :, :]
    from_real = jnp.stack([real_part, imag_part], -3)
    from_imag = jnp.stack([-imag_part, real_part], -3)
    return jnp.stack([from_real, from_imag], -4)

def block_windows(signal, block_len, lead_blocks, span_blocks, out_blocks):
    total_blocks = out_blocks + span_blocks - 1
    right_pad = total_blocks * block_len - lead_blocks * block_len - signal.shape[-1]
    padded = jnp.pad(signal, [(0, 0)] * (signal.ndim - 1) + [(lead_blocks * block_len, right_pad)])
    blocked = padded.reshape(signal.shape[:-1] + (total_blocks, block_len))
    return jnp.concatenate([blocked[..., offset_block:offset_block + out_blocks, :] for offset_block in range(span_blocks)], -1)

def chirp_taps(counts, sweep_rates, longest):
    position = jnp.arange(longest, dtype=jnp.int32)[None, :]
    lengths = counts[:, None]
    shifted = position - (longest // 2 - lengths // 2)
    inside = (shifted >= 0) & (shifted < lengths)
    extent = lengths.astype(jnp.float32)
    located = shifted.astype(jnp.float32)
    centred = (located - 0.5 * (extent - 1.0)) / extent
    angles = jnp.pi * sweep_rates[:, None] * extent * centred * centred
    envelope = (0.5 - 0.5 * jnp.cos(2.0 * jnp.pi * (located + 0.5) / extent)) * 1.6 / jnp.sqrt(extent)
    envelope = jnp.where(inside, envelope, jnp.zeros_like(envelope))
    return jnp.stack([envelope * jnp.cos(angles), envelope * jnp.sin(angles)], 1)

def azimuth_focus(columns, coeffs):
    block_len = coeffs.shape[-1] // 8
    pulses = columns.shape[-1]
    out_blocks = -(-pulses // block_len)
    windows = block_windows(columns, block_len, 4, 9, out_blocks)
    matrices = complex_matrix(toeplitz_rows(coeffs, block_len, 9 * block_len))
    product = jnp.einsum('sanw,saeiw->seni', windows, matrices)
    return product.reshape(columns.shape[:-1] + (out_blocks * block_len,))[..., :pulses]

def reference(raw_echoes, range_taps, beam_weights, channel_order, group_cells, tap_counts, chirp_rates):
    filters = jnp.take(range_taps, channel_order, axis=0).astype(jnp.float32)
    weights = jnp.take(beam_weights, channel_order, axis=0).astype(jnp.float32)
    block_len = L // 2
    matrices = complex_matrix(toeplitz_rows(filters, block_len, 3 * block_len))

    def pulse_block(echoes):
        windows = block_windows(echoes.astype(jnp.float32), block_len, 1, 3, R // block_len)
        spectra = jnp.einsum('pcanw,caeiw->pceni', windows, matrices).reshape(echoes.shape)
        real_term = spectra[:, :, 0] * weights[:, 0] - spectra[:, :, 1] * weights[:, 1]
        imag_term = spectra[:, :, 0] * weights[:, 1] + spectra[:, :, 1] * weights[:, 0]
        channel_terms = jnp.stack([real_term, imag_term], 2)
        grouped = lax.optimization_barrier(jnp.sum(channel_terms.reshape(channel_terms.shape[0], N_CHAN, CH_DEV, 2, R), 2))
        grouped = lax.optimization_barrier(grouped.astype(jnp.bfloat16)).astype(jnp.float32)
        return lax.optimization_barrier(jnp.sum(grouped, 1)).astype(jnp.bfloat16)
    beamed = lax.map(pulse_block, raw_echoes.reshape(N_TILE, PUL_DEV, C, 2, R)).reshape(P_SIZE, 2, R)
    columns = beamed.transpose(2, 1, 0)
    all_taps = chirp_taps(tap_counts, chirp_rates, KMAX).astype(jnp.bfloat16)

    def cell_block(cell_group):
        return azimuth_focus(cell_group[0].astype(jnp.float32), cell_group[1].astype(jnp.float32))
    focused = lax.map(cell_block, (columns.reshape(R // SHARE, SHARE, 2, P_SIZE), all_taps.reshape(R // SHARE, SHARE, 2, KMAX))).reshape(R, 2, P_SIZE)
    group_starts = (jnp.cumsum(group_cells) - group_cells).astype(jnp.int32)
    padded = jnp.pad(focused, ((0, MAXG), (0, 0), (0, 0)))

    def one_group(start_cell, size_cells):
        window_cut = lax.dynamic_slice_in_dim(padded, start_cell, MAXG, 0)
        inside = jnp.arange(MAXG, dtype=jnp.int32) < size_cells
        return jnp.where(inside[:, None, None], window_cut, jnp.zeros_like(window_cut))
    return jax.vmap(one_group)(group_starts, group_cells).reshape(SLOTS, 2, P_SIZE)
```

```python
import functools

import jax
import jax.numpy as jnp
import numpy as np
from jax import lax
from jax.experimental import pallas as pl
from jax.experimental.pallas import tpu as pltpu
from jax.sharding import PartitionSpec as P

KMAX = 640


def toeplitz_rows(coeffs, block_len, span_len):
    leading = coeffs.shape[:-1]
    filler = jnp.zeros(leading + (span_len + 1 - coeffs.shape[-1],), coeffs.dtype)
    extended = jnp.concatenate([coeffs, filler], -1)
    repeated = jnp.tile(extended, (1,) * len(leading) + (block_len,))
    return repeated[..., : block_len * span_len].reshape(leading + (block_len, span_len))


def complex_matrix(toeplitz_pair):
    real_part = toeplitz_pair[..., 0, :, :]
    imag_part = toeplitz_pair[..., 1, :, :]
    from_real = jnp.stack([real_part, imag_part], -3)
    from_imag = jnp.stack([-imag_part, real_part], -3)
    return jnp.stack([from_real, from_imag], -4)


def block_windows(signal, block_len, lead_blocks, span_blocks, out_blocks):
    total_blocks = out_blocks + span_blocks - 1
    right_pad = total_blocks * block_len - lead_blocks * block_len - signal.shape[-1]
    padded = jnp.pad(signal, [(0, 0)] * (signal.ndim - 1) + [(lead_blocks * block_len, right_pad)])
    blocked = padded.reshape(signal.shape[:-1] + (total_blocks, block_len))
    return jnp.concatenate(
        [
            blocked[..., offset_block : offset_block + out_blocks, :]
            for offset_block in range(span_blocks)
        ],
        -1,
    )


def chirp_taps(counts, sweep_rates, longest):
    position = jnp.arange(longest, dtype=jnp.int32)[None, :]
    lengths = counts[:, None]
    shifted = position - (longest // 2 - lengths // 2)
    inside = (shifted >= 0) & (shifted < lengths)
    extent = lengths.astype(jnp.float32)
    located = shifted.astype(jnp.float32)
    centred = (located - 0.5 * (extent - 1.0)) / extent
    angles = jnp.pi * sweep_rates[:, None] * extent * centred * centred
    envelope = (
        (0.5 - 0.5 * jnp.cos(2.0 * jnp.pi * (located + 0.5) / extent)) * 1.6 / jnp.sqrt(extent)
    )
    envelope = jnp.where(inside, envelope, jnp.zeros_like(envelope))
    return jnp.stack([envelope * jnp.cos(angles), envelope * jnp.sin(angles)], 1)


def range_compress(echoes, filters):
    block_len = filters.shape[-1] // 2
    windows = block_windows(echoes, block_len, 1, 3, echoes.shape[-1] // block_len)
    matrices = complex_matrix(toeplitz_rows(filters, block_len, 3 * block_len))
    product = jnp.einsum(
        "pcanw,caeiw->pceni", windows, matrices, preferred_element_type=jnp.float32
    )
    return product.reshape(echoes.shape)


def azimuth_focus(columns, coeffs):
    block_len = coeffs.shape[-1] // 8
    pulses = columns.shape[-1]
    out_blocks = -(-pulses // block_len)
    windows = block_windows(columns, block_len, 4, 9, out_blocks)
    matrices = complex_matrix(toeplitz_rows(coeffs, block_len, 9 * block_len))
    product = jnp.einsum("sanw,saeiw->seni", windows, matrices, preferred_element_type=jnp.float32)
    return product.reshape(columns.shape[:-1] + (out_blocks * block_len,))[..., :pulses]


def owner_slots(signal, group_starts, group_sizes, offset, slot_width, margin):
    padded = jnp.pad(signal, [(0, 0)] * (signal.ndim - 1) + [(0, margin)])

    def one_group(start_cell, size_cells):
        window_cut = lax.dynamic_slice_in_dim(
            padded, start_cell + offset, slot_width, signal.ndim - 1
        )
        inside = jnp.arange(slot_width, dtype=jnp.int32) + offset < size_cells
        return jnp.where(inside, window_cut, jnp.zeros_like(window_cut))

    return jax.vmap(one_group)(group_starts, group_sizes)


def generic_device(
    raw_echoes, range_taps, beam_weights, channel_order, group_cells, tap_counts, chirp_rates
):
    local_chans = raw_echoes.shape[1]
    all_chans = range_taps.shape[0]
    first_slot = lax.axis_index("chan") * local_chans
    own_channels = lax.dynamic_slice_in_dim(channel_order, first_slot, local_chans)
    selector = (own_channels[:, None] == jnp.arange(all_chans, dtype=jnp.int32)[None, :]).astype(
        jnp.bfloat16
    )
    filters = jnp.dot(
        selector, range_taps.reshape(all_chans, -1), preferred_element_type=jnp.float32
    )
    filters = filters.astype(jnp.bfloat16).reshape(local_chans, 2, -1)
    weights = jnp.dot(
        selector, beam_weights.reshape(all_chans, -1), preferred_element_type=jnp.float32
    )
    weights = weights.reshape(local_chans, 2, -1)
    spectra = range_compress(raw_echoes, filters)
    real_sum = jnp.sum(spectra[:, :, 0] * weights[:, 0] - spectra[:, :, 1] * weights[:, 1], 1)
    imag_sum = jnp.sum(spectra[:, :, 0] * weights[:, 1] + spectra[:, :, 1] * weights[:, 0], 1)
    partial_value = jnp.stack([real_sum, imag_sum], 1)
    tile_count = group_cells.shape[0]
    cell_count = raw_echoes.shape[-1]
    average = cell_count // tile_count
    capacity = average + average // 2
    chan_ways = lax.axis_size("chan")
    half_cap = capacity // chan_ways
    group_starts = jnp.cumsum(group_cells) - group_cells
    chan_offset = lax.axis_index("chan") * half_cap
    summed = lax.psum(partial_value.astype(jnp.bfloat16), "chan")
    outgoing = owner_slots(summed, group_starts, group_cells, chan_offset, half_cap, capacity)
    outgoing = outgoing.transpose(0, 3, 2, 1)
    incoming = lax.all_to_all(outgoing, "tile", split_axis=0, concat_axis=3, tiled=True)
    columns = incoming[0]
    tile_here = lax.axis_index("tile")
    begin_cell = lax.dynamic_index_in_dim(group_starts, tile_here, keepdims=False)
    owned_cells = lax.dynamic_index_in_dim(group_cells, tile_here, keepdims=False)
    local_slot = chan_offset + jnp.arange(half_cap, dtype=jnp.int32)
    inside = local_slot < owned_cells
    count_table = jnp.pad(tap_counts, (0, capacity), mode="edge")
    rate_table = jnp.pad(chirp_rates, (0, capacity), mode="edge")
    count_here = lax.dynamic_slice_in_dim(count_table, begin_cell + chan_offset, half_cap)
    rate_here = lax.dynamic_slice_in_dim(rate_table, begin_cell + chan_offset, half_cap)
    taps_here = chirp_taps(count_here, rate_here, KMAX)
    taps_here = jnp.where(inside[:, None, None], taps_here, jnp.zeros_like(taps_here)).astype(
        jnp.bfloat16
    )
    return azimuth_focus(columns, taps_here)


MESH = pl.DeviceIdType.MESH
BLOCK = 128
SPAN = 6 * BLOCK
STEPS = 5


def split_bf16(matrix):
    high = matrix.astype(jnp.bfloat16)
    low = (matrix - high.astype(np.float64)).astype(jnp.bfloat16)
    return np.stack([high, low])


def fourier_tables(pulses, local):
    points = 2 * pulses
    freq = np.arange(points)[:, None]
    unit = 2.0 * np.pi / points

    def rotation(index, sign):
        angle = unit * ((freq * index[None, :]) % points)
        return np.cos(angle), sign * np.sin(angle)

    cos_x, sin_x = rotation(np.arange(pulses), -1.0)
    forward = np.stack(
        [np.concatenate([cos_x, sin_x]).T, np.concatenate([-sin_x, cos_x]).T]
    ).reshape(2, -1, 2, 1, local, 2 * points)
    forward = np.broadcast_to(forward, forward.shape[:3] + (2,) + forward.shape[4:])
    forward = forward.transpose(1, 0, 2, 3, 4, 5).reshape(-1, 2 * points)
    cos_h, sin_h = rotation(pulses - np.arange(points), -1.0)
    taps = np.block([[cos_h, -sin_h], [sin_h, cos_h]])
    cos_y, sin_y = rotation(np.arange(pulses), 1.0)
    inverse = np.block([[cos_y, sin_y], [-sin_y, cos_y]]) / points
    return forward.astype(jnp.bfloat16), split_bf16(taps), inverse.astype(jnp.bfloat16)


def even_series(square, terms):
    value = jnp.full_like(square, terms[-1])
    for term in reversed(terms[:-1]):
        value = value * square + term
    return value


COS_TERMS = [(-1.0) ** n * (2 * np.pi) ** (2 * n) / float(np.prod(np.arange(1, 2 * n + 1, dtype=np.float64))) for n in range(9)]
SIN_TERMS = [(-1.0) ** n * (2 * np.pi) ** (2 * n + 1) / float(np.prod(np.arange(1, 2 * n + 2, dtype=np.float64))) for n in range(9)]


def write_taps(extent, rate, scale, tap_ref, first_tap):
    rows = tap_ref.shape[0] // 2
    length = extent.astype(jnp.int32)
    start = KMAX // 2 - length // 2
    inverse = 1.0 / extent
    turn = 0.5 * rate * extent
    for at in range(0, rows, 32):
        tap = lax.broadcasted_iota(jnp.int32, (32, 2 * BLOCK), 0) + (first_tap + at)
        shifted = tap - start
        inside = (shifted >= 0) & (shifted < length)
        centred = (shifted.astype(jnp.float32) - 0.5 * (extent - 1.0)) * inverse
        square = centred * centred
        envelope = jnp.where(inside, scale * (0.5 + 0.5 * even_series(square, COS_TERMS)), 0.0)
        turns = turn * square
        turns = turns - jnp.floor(turns + 0.5)
        turn_square = turns * turns
        real = envelope * even_series(turn_square, COS_TERMS)
        imag = envelope * (turns * even_series(turn_square, SIN_TERMS))
        tap_ref[at : at + 32] = real.astype(jnp.bfloat16)
        tap_ref[rows + at : rows + at + 32] = imag.astype(jnp.bfloat16)


def focus_kernel(
    half_cap,
    order_hbm,
    cells_hbm,
    raw_ref,
    filter_ref,
    weight_ref,
    count_ref,
    rate_ref,
    forward_ref,
    spectrum_ref,
    inverse_ref,
    out_ref,
    order_ref,
    cells_ref,
    raw,
    filters,
    weights,
    counts,
    rates,
    forward,
    spectrum,
    inverse,
    mirror,
    spread,
    blocks,
    matrices,
    real_sum,
    imag_sum,
    packed,
    columns,
    tap_ref,
    turned,
    load_sems,
    raw_sems,
    send_sems,
    recv_sems,
):
    tiles = packed.shape[0]
    tile_here = lax.axis_index("tile")
    chan_here = lax.axis_index("chan")
    here = 2 * tile_here + chan_here
    local_chans, local, pieces, _ = raw.shape
    out_blocks = pieces // 2
    rows = out_blocks * local
    pulses = tiles * local
    points = 2 * pulses
    barrier = pltpu.get_barrier_semaphore()
    for hop in range(1, 2 * tiles):
        peer = lax.rem(here + hop, 2 * tiles)
        pl.semaphore_signal(
            barrier,
            inc=1,
            device_id={"tile": peer // 2, "chan": lax.rem(peer, 2)},
            device_id_type=MESH,
        )

    def fetch(source, target, at):
        return pltpu.make_async_copy(source, target, load_sems.at[at])

    def fetch_raw(chan):
        return pltpu.make_async_copy(raw_ref.at[:, chan], raw.at[chan], raw_sems.at[chan])

    get_filters = fetch(filter_ref, filters, 0)
    get_weights = fetch(weight_ref, weights, 1)
    late = [
        fetch(count_ref, counts, 2),
        fetch(rate_ref, rates, 3),
        fetch(spectrum_ref, spectrum, 4),
        fetch(forward_ref, forward, 5),
        fetch(inverse_ref, inverse, 6),
    ]
    get_order = fetch(order_hbm, order_ref, 7)
    get_cells = fetch(cells_hbm, cells_ref, 8)
    get_order.start()
    get_filters.start()
    for chan in range(local_chans):
        fetch_raw(chan).start()
    get_weights.start()
    get_cells.start()
    for copy in late:
        copy.start()

    edge = jnp.zeros((local_chans, 2, local, 2 * BLOCK), jnp.bfloat16)
    blocks[:, :2] = edge
    blocks[:, out_blocks + 2 :] = edge
    row = lax.broadcasted_iota(jnp.int32, (2 * BLOCK, 2 * BLOCK), 0)
    lane = lax.broadcasted_iota(jnp.int32, (2 * BLOCK, 2 * BLOCK), 1)
    mirror[...] = jnp.where(row + lane == 2 * BLOCK - 1, 1.0, 0.0).astype(jnp.bfloat16)
    get_order.wait()
    get_filters.wait()

    physical = [order_ref[chan_here * local_chans + chan] for chan in range(local_chans)]
    own = jnp.concatenate([filters[at].astype(jnp.float32) for at in physical], 0)
    own = own.astype(jnp.bfloat16)
    backward = jnp.concatenate(
        [
            jnp.dot(own[:, 2 * BLOCK :], mirror[...], preferred_element_type=jnp.float32),
            jnp.dot(own[:, : 2 * BLOCK], mirror[...], preferred_element_type=jnp.float32),
            jnp.zeros((2 * local_chans, 2 * BLOCK), jnp.float32),
        ],
        1,
    )
    for chan in range(local_chans):

        def toeplitz(part):
            at = 2 * chan + part
            row = jnp.broadcast_to(backward[at : at + 1], (BLOCK, SPAN))
            return pltpu.roll(row, 1, 1, stride=1, stride_axis=0)

        real_rows = toeplitz(0)
        imag_rows = toeplitz(1)
        for step in range(STEPS):
            at = slice((4 - step) * BLOCK, (5 - step) * BLOCK)
            real = real_rows[:, at].astype(jnp.bfloat16)
            imag = imag_rows[:, at]
            top = 2 * step * BLOCK
            matrices[chan, top : top + BLOCK, :BLOCK] = real
            matrices[chan, top : top + BLOCK, BLOCK:] = imag.astype(jnp.bfloat16)
            matrices[chan, top + BLOCK : top + 2 * BLOCK, :BLOCK] = (-imag).astype(jnp.bfloat16)
            matrices[chan, top + BLOCK : top + 2 * BLOCK, BLOCK:] = real

    for chan in range(local_chans):
        fetch_raw(chan).wait()
        if chan == 0:
            get_weights.wait()
            get_cells.wait()
        spread[chan] = raw[chan].reshape(local * pieces, BLOCK).astype(jnp.float32)
        for block in range(out_blocks):
            for part in range(2):
                piece = spread[chan, pl.ds(2 * block + part, local, stride=pieces), :]
                blocks[chan, block + 2, :, part * BLOCK : (part + 1) * BLOCK] = piece.astype(
                    jnp.bfloat16
                )
        total = None
        for step in range(STEPS):
            window = blocks[chan, step : step + out_blocks].reshape(rows, 2 * BLOCK)
            matrix = matrices[chan, 2 * step * BLOCK : 2 * (step + 1) * BLOCK]
            term = jnp.dot(window, matrix, preferred_element_type=jnp.float32)
            total = term if total is None else total + term
        own_weight = weights[physical[chan]].astype(jnp.float32)
        for block in range(out_blocks):
            cells = slice(block * BLOCK, (block + 1) * BLOCK)
            weight_real = own_weight[0:1, cells]
            weight_imag = own_weight[1:2, cells]
            real = total[block * local : (block + 1) * local, :BLOCK]
            imag = total[block * local : (block + 1) * local, BLOCK:]
            new_real = weight_real * real - weight_imag * imag
            new_imag = weight_imag * real + weight_real * imag
            if chan > 0:
                new_real += real_sum[block]
                new_imag += imag_sum[block]
            real_sum[block] = new_real
            imag_sum[block] = new_imag

    is_left = lax.broadcasted_iota(jnp.int32, (local, BLOCK), 1) < BLOCK // 2

    def pack(tile, real, imag):
        def put(chan, at):
            cells = slice(at * BLOCK, (at + 1) * BLOCK)
            packed[tile, chan, 0] = real[:, cells].astype(jnp.bfloat16)
            packed[tile, chan, 1] = imag[:, cells].astype(jnp.bfloat16)

        put(0, 0)
        put(1, 2)
        half_real, half_imag = real[:, BLOCK : 2 * BLOCK], imag[:, BLOCK : 2 * BLOCK]
        packed[tile, 0, 2] = jnp.where(
            is_left, half_real, pltpu.roll(half_imag, BLOCK // 2, 1)
        ).astype(jnp.bfloat16)
        packed[tile, 1, 2] = jnp.where(
            is_left, pltpu.roll(half_real, BLOCK // 2, 1), half_imag
        ).astype(jnp.bfloat16)

    for pair in range(tiles // 2):
        first = cells_ref[2 * pair]
        real = jnp.concatenate([real_sum[4 * pair + at] for at in range(4)], 1)
        imag = jnp.concatenate([imag_sum[4 * pair + at] for at in range(4)], 1)
        pack(2 * pair, real, imag)
        both = pltpu.roll(jnp.concatenate([real, imag], 0), 4 * BLOCK - first, 1)
        pack(2 * pair + 1, both[:local], both[local:])

    pl.semaphore_wait(barrier, 2 * tiles - 1)
    copies = []
    for hop in range(2 * tiles - 1):
        peer = hop + jnp.where(hop >= here, 1, 0)
        copy = pltpu.make_async_remote_copy(
            src_ref=packed.at[peer // 2, lax.rem(peer, 2)],
            dst_ref=columns.at[tile_here // 2, :, 2 * lax.rem(tile_here, 2) + chan_here],
            send_sem=send_sems.at[hop],
            recv_sem=recv_sems.at[here],
            device_id={"tile": peer // 2, "chan": lax.rem(peer, 2)},
            device_id_type=MESH,
        )
        copy.start()
        copies.append(copy)
    columns[tile_here // 2, :, 2 * lax.rem(tile_here, 2) + chan_here] = packed[
        tile_here, chan_here
    ]
    for copy in late:
        copy.wait()
    begin = 0
    for tile in range(tiles):
        begin += jnp.where(tile < tile_here, cells_ref[tile], 0)
    cell_count = counts.shape[1]

    def own_cells(table):
        wide = jnp.broadcast_to(table.astype(jnp.float32), (8, cell_count))

        def cut(at):
            shift = lax.rem(2 * cell_count - begin - at, cell_count)
            return pltpu.roll(wide, shift, 1)[0:1, :BLOCK]

        return jnp.concatenate([cut(2 * BLOCK * chan_here), cut(BLOCK + BLOCK // 2 * chan_here)], 1)

    extent = own_cells(counts[...])
    place = lax.broadcasted_iota(jnp.int32, (1, 2 * BLOCK), 1)
    place += jnp.where(place < BLOCK, 2 * BLOCK * chan_here, BLOCK // 2 * chan_here)
    live = place < cells_ref[tile_here]
    scale = jnp.where(live, 1.6 / jnp.sqrt(extent), 0.0)
    rate = own_cells(rates[...])
    write_taps(extent, rate, scale, tap_ref, KMAX // 2 - pulses)
    taps = tap_ref[...]
    response = jnp.dot(spectrum[0], taps, preferred_element_type=jnp.float32) + jnp.dot(
        spectrum[1], taps, preferred_element_type=jnp.float32
    )
    turned[...] = response.T

    image = None
    for half in range(2):
        parts = []
        for group in (2 * half, 2 * half + 1):
            for at in range(4):
                source = 4 * group + at

                @pl.when(source != here)
                def _():
                    pltpu.make_async_remote_copy(
                        src_ref=packed.at[source // 2, source % 2],
                        dst_ref=columns.at[group, :, at],
                        send_sem=send_sems.at[0],
                        recv_sem=recv_sems.at[source],
                        device_id={"tile": source // 2, "chan": source % 2},
                        device_id_type=MESH,
                    ).wait_recv()

            whole = columns[group, :2].reshape(BLOCK, BLOCK).T
            folded = columns[group, 2].reshape(BLOCK // 2, BLOCK).astype(jnp.float32).T
            folded = jnp.concatenate([folded[: BLOCK // 2], folded[BLOCK // 2 :]], 1)
            parts.append(jnp.concatenate([whole, folded.astype(jnp.bfloat16)], 0))
        term = jnp.dot(
            jnp.concatenate(parts, 1),
            forward[2 * half * BLOCK : 2 * (half + 1) * BLOCK],
            preferred_element_type=jnp.float32,
        )
        image = term if image is None else image + term
    slots = image.shape[0]
    real, imag = image[:, :points], image[:, points:]
    tap_real, tap_imag = turned[:slots, :points], turned[:slots, points:]
    product = jnp.concatenate(
        [real * tap_real - imag * tap_imag, real * tap_imag + imag * tap_real], 1
    ).astype(jnp.bfloat16)
    result = jnp.dot(product, inverse[...], preferred_element_type=jnp.float32)
    for part in range(2):
        lanes = slice(part * pulses, (part + 1) * pulses)
        out_ref[pl.ds(BLOCK * chan_here + part, BLOCK, stride=2), :] = result[:BLOCK, lanes]
        out_ref[pl.ds(2 * BLOCK * (1 - chan_here) + part, slots - BLOCK, stride=2), :] = result[
            BLOCK:, lanes
        ]
    for copy in copies:
        copy.wait_send()


def focus_call(raw_echoes, range_taps, beam_weights, order, cells, counts, rates, half_cap):
    local, local_chans, _, cell_count = raw_echoes.shape
    tiles = cells.shape[0]
    pulses = tiles * local
    out_blocks = cell_count // BLOCK
    raw_echoes = raw_echoes.reshape(local, local_chans, 2, out_blocks, BLOCK)
    raw_echoes = raw_echoes.transpose(0, 1, 3, 2, 4).reshape(local, local_chans, -1, BLOCK)
    tables = [jnp.asarray(table) for table in fourier_tables(pulses, local)]
    counts, rates = counts[None], rates[None]
    arrays = [raw_echoes, range_taps, beam_weights, counts, rates] + tables
    total = pltpu.VMEM((out_blocks, local, BLOCK), jnp.float32)
    result = pl.pallas_call(
        functools.partial(focus_kernel, half_cap),
        out_shape=pltpu.VMEM((2 * half_cap, pulses), jnp.float32),
        in_specs=[pl.BlockSpec(memory_space=pl.ANY)] * (2 + len(arrays)),
        out_specs=pl.BlockSpec(memory_space=pltpu.VMEM),
        scratch_shapes=[pltpu.SMEM(order.shape, order.dtype), pltpu.SMEM(cells.shape, cells.dtype)]
        + [pltpu.VMEM((local_chans, local, 2 * out_blocks, BLOCK), raw_echoes.dtype)]
        + [pltpu.VMEM(array.shape, array.dtype) for array in arrays[1:]]
        + [
            pltpu.VMEM((2 * BLOCK, 2 * BLOCK), jnp.bfloat16),
            pltpu.VMEM((local_chans, local * 2 * out_blocks, BLOCK), jnp.float32),
            pltpu.VMEM((local_chans, out_blocks + 4, local, 2 * BLOCK), jnp.bfloat16),
            pltpu.VMEM((local_chans, 2 * STEPS * BLOCK, 2 * BLOCK), jnp.bfloat16),
            total,
            total,
            pltpu.VMEM((tiles, 2, 3, local, BLOCK), jnp.bfloat16),
            pltpu.VMEM((tiles // 2, 3, 4, local, BLOCK), jnp.bfloat16),
            pltpu.VMEM((4 * pulses, 2 * BLOCK), jnp.bfloat16),
            pltpu.VMEM((2 * BLOCK, 4 * pulses), jnp.float32),
            pltpu.SemaphoreType.DMA((len(arrays) + 1,)),
            pltpu.SemaphoreType.DMA((local_chans,)),
            pltpu.SemaphoreType.DMA((2 * tiles,)),
            pltpu.SemaphoreType.DMA((2 * tiles,)),
        ],
        compiler_params=pltpu.CompilerParams(
            collective_id=0, has_side_effects=True, vmem_limit_bytes=56 << 20
        ),
    )(order, cells, *arrays)
    return result.reshape(half_cap, 2, pulses)


def on_device(
    raw_echoes, range_taps, beam_weights, channel_order, group_cells, tap_counts, chirp_rates
):
    tiles = group_cells.shape[0]
    local, _, _, cell_count = raw_echoes.shape
    average = cell_count // tiles
    half_cap = (average + average // 2) // lax.axis_size("chan")
    fits = average == 2 * BLOCK and lax.axis_size("chan") == 2 and local == 16 and tiles == 8
    if not fits or range_taps.shape[-1] != 4 * BLOCK:
        return generic_device(
            raw_echoes,
            range_taps,
            beam_weights,
            channel_order,
            group_cells,
            tap_counts,
            chirp_rates,
        )
    return focus_call(
        raw_echoes,
        range_taps,
        beam_weights,
        channel_order,
        group_cells,
        tap_counts,
        chirp_rates,
        half_cap,
    )


def solution(mesh):
    return jax.shard_map(
        on_device,
        mesh=mesh,
        in_specs=(P(("scene", "tile"), "chan", None, None), P(), P(), P(), P(), P(), P()),
        out_specs=P(("scene", "tile", "chan"), None, None),
        check_vma=False,
    )
```

```python
import functools

import jax
import jax.numpy as jnp
import numpy as np
from jax import lax
from jax.experimental import pallas as pl
from jax.experimental.pallas import tpu as pltpu
from jax.sharding import PartitionSpec as P

KMAX = 640


def toeplitz_rows(coeffs, block_len, span_len):
    leading = coeffs.shape[:-1]
    filler = jnp.zeros(leading + (span_len + 1 - coeffs.shape[-1],), coeffs.dtype)
    extended = jnp.concatenate([coeffs, filler], -1)
    repeated = jnp.tile(extended, (1,) * len(leading) + (block_len,))
    return repeated[..., : block_len * span_len].reshape(leading + (block_len, span_len))


def complex_matrix(toeplitz_pair):
    real_part = toeplitz_pair[..., 0, :, :]
    imag_part = toeplitz_pair[..., 1, :, :]
    from_real = jnp.stack([real_part, imag_part], -3)
    from_imag = jnp.stack([-imag_part, real_part], -3)
    return jnp.stack([from_real, from_imag], -4)


def block_windows(signal, block_len, lead_blocks, span_blocks, out_blocks):
    total_blocks = out_blocks + span_blocks - 1
    right_pad = total_blocks * block_len - lead_blocks * block_len - signal.shape[-1]
    padded = jnp.pad(signal, [(0, 0)] * (signal.ndim - 1) + [(lead_blocks * block_len, right_pad)])
    blocked = padded.reshape(signal.shape[:-1] + (total_blocks, block_len))
    return jnp.concatenate(
        [
            blocked[..., offset_block : offset_block + out_blocks, :]
            for offset_block in range(span_blocks)
        ],
        -1,
    )


def chirp_taps(counts, sweep_rates, longest):
    position = jnp.arange(longest, dtype=jnp.int32)[None, :]
    lengths = counts[:, None]
    shifted = position - (longest // 2 - lengths // 2)
    inside = (shifted >= 0) & (shifted < lengths)
    extent = lengths.astype(jnp.float32)
    located = shifted.astype(jnp.float32)
    centred = (located - 0.5 * (extent - 1.0)) / extent
    angles = jnp.pi * sweep_rates[:, None] * extent * centred * centred
    envelope = (
        (0.5 - 0.5 * jnp.cos(2.0 * jnp.pi * (located + 0.5) / extent)) * 1.6 / jnp.sqrt(extent)
    )
    envelope = jnp.where(inside, envelope, jnp.zeros_like(envelope))
    return jnp.stack([envelope * jnp.cos(angles), envelope * jnp.sin(angles)], 1)


def range_compress(echoes, filters):
    block_len = filters.shape[-1] // 2
    windows = block_windows(echoes, block_len, 1, 3, echoes.shape[-1] // block_len)
    matrices = complex_matrix(toeplitz_rows(filters, block_len, 3 * block_len))
    product = jnp.einsum(
        "pcanw,caeiw->pceni", windows, matrices, preferred_element_type=jnp.float32
    )
    return product.reshape(echoes.shape)


def azimuth_focus(columns, coeffs):
    block_len = coeffs.shape[-1] // 8
    pulses = columns.shape[-1]
    out_blocks = -(-pulses // block_len)
    windows = block_windows(columns, block_len, 4, 9, out_blocks)
    matrices = complex_matrix(toeplitz_rows(coeffs, block_len, 9 * block_len))
    product = jnp.einsum("sanw,saeiw->seni", windows, matrices, preferred_element_type=jnp.float32)
    return product.reshape(columns.shape[:-1] + (out_blocks * block_len,))[..., :pulses]


def owner_slots(signal, group_starts, group_sizes, offset, slot_width, margin):
    padded = jnp.pad(signal, [(0, 0)] * (signal.ndim - 1) + [(0, margin)])

    def one_group(start_cell, size_cells):
        window_cut = lax.dynamic_slice_in_dim(
            padded, start_cell + offset, slot_width, signal.ndim - 1
        )
        inside = jnp.arange(slot_width, dtype=jnp.int32) + offset < size_cells
        return jnp.where(inside, window_cut, jnp.zeros_like(window_cut))

    return jax.vmap(one_group)(group_starts, group_sizes)


def generic_device(
    raw_echoes, range_taps, beam_weights, channel_order, group_cells, tap_counts, chirp_rates
):
    local_chans = raw_echoes.shape[1]
    all_chans = range_taps.shape[0]
    first_slot = lax.axis_index("chan") * local_chans
    own_channels = lax.dynamic_slice_in_dim(channel_order, first_slot, local_chans)
    selector = (own_channels[:, None] == jnp.arange(all_chans, dtype=jnp.int32)[None, :]).astype(
        jnp.bfloat16
    )
    filters = jnp.dot(
        selector, range_taps.reshape(all_chans, -1), preferred_element_type=jnp.float32
    )
    filters = filters.astype(jnp.bfloat16).reshape(local_chans, 2, -1)
    weights = jnp.dot(
        selector, beam_weights.reshape(all_chans, -1), preferred_element_type=jnp.float32
    )
    weights = weights.reshape(local_chans, 2, -1)
    spectra = range_compress(raw_echoes, filters)
    real_sum = jnp.sum(spectra[:, :, 0] * weights[:, 0] - spectra[:, :, 1] * weights[:, 1], 1)
    imag_sum = jnp.sum(spectra[:, :, 0] * weights[:, 1] + spectra[:, :, 1] * weights[:, 0], 1)
    partial_value = jnp.stack([real_sum, imag_sum], 1)
    tile_count = group_cells.shape[0]
    cell_count = raw_echoes.shape[-1]
    average = cell_count // tile_count
    capacity = average + average // 2
    chan_ways = lax.axis_size("chan")
    half_cap = capacity // chan_ways
    group_starts = jnp.cumsum(group_cells) - group_cells
    chan_offset = lax.axis_index("chan") * half_cap
    summed = lax.psum(partial_value.astype(jnp.bfloat16), "chan")
    outgoing = owner_slots(summed, group_starts, group_cells, chan_offset, half_cap, capacity)
    outgoing = outgoing.transpose(0, 3, 2, 1)
    incoming = lax.all_to_all(outgoing, "tile", split_axis=0, concat_axis=3, tiled=True)
    columns = incoming[0]
    tile_here = lax.axis_index("tile")
    begin_cell = lax.dynamic_index_in_dim(group_starts, tile_here, keepdims=False)
    owned_cells = lax.dynamic_index_in_dim(group_cells, tile_here, keepdims=False)
    local_slot = chan_offset + jnp.arange(half_cap, dtype=jnp.int32)
    inside = local_slot < owned_cells
    count_table = jnp.pad(tap_counts, (0, capacity), mode="edge")
    rate_table = jnp.pad(chirp_rates, (0, capacity), mode="edge")
    count_here = lax.dynamic_slice_in_dim(count_table, begin_cell + chan_offset, half_cap)
    rate_here = lax.dynamic_slice_in_dim(rate_table, begin_cell + chan_offset, half_cap)
    taps_here = chirp_taps(count_here, rate_here, KMAX)
    taps_here = jnp.where(inside[:, None, None], taps_here, jnp.zeros_like(taps_here)).astype(
        jnp.bfloat16
    )
    return azimuth_focus(columns, taps_here)


MESH = pl.DeviceIdType.MESH
BLOCK = 128
SPAN = 6 * BLOCK
STEPS = 5


def split_bf16(matrix):
    high = matrix.astype(jnp.bfloat16)
    low = (matrix - high.astype(np.float64)).astype(jnp.bfloat16)
    return np.stack([high, low])


def fourier_tables(pulses, local):
    points = 2 * pulses
    freq = np.arange(points)[:, None]
    unit = 2.0 * np.pi / points

    def rotation(index, sign):
        angle = unit * ((freq * index[None, :]) % points)
        return np.cos(angle), sign * np.sin(angle)

    cos_x, sin_x = rotation(np.arange(pulses), -1.0)
    forward = np.stack(
        [np.concatenate([cos_x, sin_x]).T, np.concatenate([-sin_x, cos_x]).T]
    ).reshape(2, -1, 2, 1, local, 2 * points)
    forward = np.broadcast_to(forward, forward.shape[:3] + (2,) + forward.shape[4:])
    forward = forward.transpose(1, 0, 2, 3, 4, 5).reshape(-1, 2 * points)
    cos_h, sin_h = rotation(pulses - np.arange(points), -1.0)
    taps = np.block([[cos_h, -sin_h], [sin_h, cos_h]])
    cos_y, sin_y = rotation(np.arange(pulses), 1.0)
    inverse = np.block([[cos_y, sin_y], [-sin_y, cos_y]]) / points
    inverse = np.concatenate([inverse[:points], inverse[points:]], 1)
    table = np.concatenate([forward.astype(jnp.bfloat16), *split_bf16(taps)])
    return np.concatenate([table, inverse.astype(jnp.bfloat16)])


def even_series(square, terms):
    value = jnp.full_like(square, terms[-1])
    for term in reversed(terms[:-1]):
        value = value * square + term
    return value


COS_TERMS = [(-1.0) ** n * (2 * np.pi) ** (2 * n) / float(np.prod(np.arange(1, 2 * n + 1, dtype=np.float64))) for n in range(9)]
SIN_TERMS = [(-1.0) ** n * (2 * np.pi) ** (2 * n + 1) / float(np.prod(np.arange(1, 2 * n + 2, dtype=np.float64))) for n in range(9)]


def write_taps(extent, rate, scale, tap_ref, first_tap):
    rows = tap_ref.shape[0] // 2
    length = extent.astype(jnp.int32)
    start = KMAX // 2 - length // 2
    inverse = 1.0 / extent
    turn = 0.5 * rate * extent
    for at in range(0, rows, 32):
        tap = lax.broadcasted_iota(jnp.int32, (32, 2 * BLOCK), 0) + (first_tap + at)
        shifted = tap - start
        inside = (shifted >= 0) & (shifted < length)
        centred = (shifted.astype(jnp.float32) - 0.5 * (extent - 1.0)) * inverse
        square = centred * centred
        envelope = jnp.where(inside, scale * (0.5 + 0.5 * even_series(square, COS_TERMS)), 0.0)
        turns = turn * square
        turns = turns - jnp.floor(turns + 0.5)
        turn_square = turns * turns
        real = envelope * even_series(turn_square, COS_TERMS)
        imag = envelope * (turns * even_series(turn_square, SIN_TERMS))
        tap_ref[at : at + 32] = real.astype(jnp.bfloat16)
        tap_ref[rows + at : rows + at + 32] = imag.astype(jnp.bfloat16)


def focus_kernel(
    half_cap,
    order_hbm,
    cells_hbm,
    raw_ref,
    filter_ref,
    weight_ref,
    count_ref,
    rate_ref,
    table_ref,
    out_ref,
    order_ref,
    cells_ref,
    raw,
    filters,
    weights,
    counts,
    rates,
    table,
    mirror,
    blocks,
    matrices,
    real_sum,
    imag_sum,
    packed,
    columns,
    tap_ref,
    turned,
    load_sems,
    raw_sems,
    send_sems,
    recv_sems,
):
    tiles = packed.shape[0]
    tile_here = lax.axis_index("tile")
    chan_here = lax.axis_index("chan")
    here = 2 * tile_here + chan_here
    local, local_chans, pieces, _ = raw.shape[1:]
    out_blocks = pieces
    pulses = tiles * local
    points = 2 * pulses
    def fetch(source, target, at):
        return pltpu.make_async_copy(source, target, load_sems.at[at])

    def fetch_raw(half, group):
        chans = pl.ds(2 * group, 2)
        return pltpu.make_async_copy(
            raw_ref.at[:, chans, pl.ds(half * pieces, pieces)],
            raw.at[half, :, chans],
            raw_sems.at[half * (local_chans // 2) + group],
        )

    get_filters = fetch(filter_ref, filters, 0)
    get_weights = fetch(weight_ref, weights, 1)
    late = [
        fetch(count_ref, counts, 2),
        fetch(rate_ref, rates, 3),
        fetch(table_ref, table, 4),
    ]
    get_order = fetch(order_hbm, order_ref, 5)
    get_cells = fetch(cells_hbm, cells_ref, 6)
    get_order.start()
    get_filters.start()
    for group in range(local_chans // 2):
        fetch_raw(0, group).start()
    get_weights.start()
    get_cells.start()
    for group in range(local_chans // 2):
        fetch_raw(1, group).start()
    for copy in late:
        copy.start()

    barrier = pltpu.get_barrier_semaphore()
    everyone = [(tile, chan) for tile in range(tiles) for chan in range(2)]
    for tile, chan in everyone:

        @pl.when(2 * tile + chan != here)
        def _():
            pl.semaphore_signal(
                barrier, inc=1, device_id={"tile": tile, "chan": chan}, device_id_type=MESH
            )

    edge = jnp.zeros((local_chans, 2, local, 2 * BLOCK), jnp.bfloat16)
    blocks[:, :2] = edge
    blocks[:, out_blocks + 2 :] = edge
    row = lax.broadcasted_iota(jnp.int32, (2 * BLOCK, 2 * BLOCK), 0)
    lane = lax.broadcasted_iota(jnp.int32, (2 * BLOCK, 2 * BLOCK), 1)
    mirror[...] = jnp.where(row + lane == 2 * BLOCK - 1, 1.0, 0.0).astype(jnp.bfloat16)
    get_order.wait()
    get_filters.wait()

    physical = [order_ref[chan_here * local_chans + chan] for chan in range(local_chans)]
    own = jnp.concatenate([filters[at].astype(jnp.float32) for at in physical], 0)
    own = own.astype(jnp.bfloat16)
    backward = jnp.concatenate(
        [
            jnp.dot(own[:, 2 * BLOCK :], mirror[...], preferred_element_type=jnp.float32),
            jnp.dot(own[:, : 2 * BLOCK], mirror[...], preferred_element_type=jnp.float32),
            jnp.zeros((2 * local_chans, 2 * BLOCK), jnp.float32),
        ],
        1,
    )
    def toeplitz(at):
        row = jnp.broadcast_to(backward[at : at + 1], (BLOCK, SPAN))
        return pltpu.roll(row, 1, 1, stride=1, stride_axis=0)

    def write_matrices(group):
        for chan in (2 * group, 2 * group + 1):
            real_rows = toeplitz(2 * chan)
            imag_rows = toeplitz(2 * chan + 1)
            for step in range(STEPS):
                at = slice((4 - step) * BLOCK, (5 - step) * BLOCK)
                real = real_rows[:, at].astype(jnp.bfloat16)
                imag = imag_rows[:, at]
                upper = slice(2 * step * BLOCK, (2 * step + 1) * BLOCK)
                lower = slice((2 * step + 1) * BLOCK, (2 * step + 2) * BLOCK)
                matrices[chan, upper, :BLOCK] = real
                matrices[chan, upper, BLOCK:] = imag.astype(jnp.bfloat16)
                matrices[chan, lower, :BLOCK] = (-imag).astype(jnp.bfloat16)
                matrices[chan, lower, BLOCK:] = real

    def spread_rows(half, group):
        fetch_raw(half, group).wait()
        for chan in (2 * group, 2 * group + 1):
            wide = jnp.swapaxes(raw[half, :, chan].astype(jnp.float32), 0, 1).astype(jnp.bfloat16)
            for block in range(pieces // 2):
                at = half * (pieces // 2) + block + 2
                blocks[chan, at, :, :BLOCK] = wide[2 * block]
                blocks[chan, at, :, BLOCK:] = wide[2 * block + 1]

    def compress(chan, first, last):
        total = None
        for step in range(STEPS):
            window = blocks[chan, first + step : last + step].reshape(-1, 2 * BLOCK)
            matrix = matrices[chan, 2 * step * BLOCK : 2 * (step + 1) * BLOCK]
            term = jnp.dot(window, matrix, preferred_element_type=jnp.float32)
            total = term if total is None else total + term
        return total

    def beamform(chan, first, last, total):
        own_weight = weights[physical[chan]].astype(jnp.float32)
        for block in range(first, last):
            cells = slice(block * BLOCK, (block + 1) * BLOCK)
            weight_real = own_weight[0:1, cells]
            weight_imag = own_weight[1:2, cells]
            real = total[(block - first) * local : (block - first + 1) * local, :BLOCK]
            imag = total[(block - first) * local : (block - first + 1) * local, BLOCK:]
            new_real = weight_real * real - weight_imag * imag
            new_imag = weight_imag * real + weight_real * imag
            if chan > 0:
                new_real += real_sum[block]
                new_imag += imag_sum[block]
            real_sum[block] = new_real
            imag_sum[block] = new_imag

    def phase(group, first, last):
        chans = (2 * group, 2 * group + 1)
        totals = [compress(chan, first, last) for chan in chans]
        for chan, total in zip(chans, totals):
            beamform(chan, first, last, total)

    is_left = lax.broadcasted_iota(jnp.int32, (local, BLOCK), 1) < BLOCK // 2

    def pack(tile, real, imag):
        def put(chan, at):
            cells = slice(at * BLOCK, (at + 1) * BLOCK)
            packed[tile, chan, 0] = real[:, cells].astype(jnp.bfloat16)
            packed[tile, chan, 1] = imag[:, cells].astype(jnp.bfloat16)

        put(0, 0)
        put(1, 2)
        half_real, half_imag = real[:, BLOCK : 2 * BLOCK], imag[:, BLOCK : 2 * BLOCK]
        packed[tile, 0, 2] = jnp.where(
            is_left, half_real, pltpu.roll(half_imag, BLOCK // 2, 1)
        ).astype(jnp.bfloat16)
        packed[tile, 1, 2] = jnp.where(
            is_left, pltpu.roll(half_real, BLOCK // 2, 1), half_imag
        ).astype(jnp.bfloat16)

    def send(tile, chan):
        return pltpu.make_async_remote_copy(
            src_ref=packed.at[tile, chan],
            dst_ref=columns.at[tile_here // 2, :, 2 * lax.rem(tile_here, 2) + chan_here],
            send_sem=send_sems.at[2 * tile + chan],
            recv_sem=recv_sems.at[here],
            device_id={"tile": tile, "chan": chan},
            device_id_type=MESH,
        )

    def deliver(pair):
        first = cells_ref[2 * pair]
        real = jnp.concatenate([real_sum[4 * pair + at] for at in range(4)], 1)
        imag = jnp.concatenate([imag_sum[4 * pair + at] for at in range(4)], 1)
        pack(2 * pair, real, imag)
        both = pltpu.roll(jnp.concatenate([real, imag], 0), 4 * BLOCK - first, 1)
        pack(2 * pair + 1, both[:local], both[local:])
        if pair == 0:
            pl.semaphore_wait(barrier, 2 * tiles - 1)
        for tile in (2 * pair, 2 * pair + 1):
            for chan in range(2):

                @pl.when(2 * tile + chan != here)
                def _():
                    send(tile, chan).start()

    groups = local_chans // 2
    write_matrices(0)
    get_weights.wait()
    for group in range(groups):
        spread_rows(0, group)
        if group + 1 < groups:
            write_matrices(group + 1)
        phase(group, 0, 4)

    def second_phase():
        for group in range(groups):
            spread_rows(1, group)
        for group in range(groups):
            phase(group, 4, out_blocks)

    get_cells.wait()
    early = tile_here < tiles // 2
    pl.when(early)(second_phase)
    deliver(0)
    pl.when(jnp.logical_not(early))(second_phase)
    for pair in range(1, tiles // 2):
        deliver(pair)
    columns[tile_here // 2, :, 2 * lax.rem(tile_here, 2) + chan_here] = packed[
        tile_here, chan_here
    ]
    for copy in late:
        copy.wait()
    begin = 0
    for tile in range(tiles):
        begin += jnp.where(tile < tile_here, cells_ref[tile], 0)
    cell_count = counts.shape[1]

    def own_cells(table):
        wide = jnp.broadcast_to(table.astype(jnp.float32), (8, cell_count))

        def cut(at):
            shift = lax.rem(2 * cell_count - begin - at, cell_count)
            return pltpu.roll(wide, shift, 1)[0:1, :BLOCK]

        return jnp.concatenate([cut(2 * BLOCK * chan_here), cut(BLOCK + BLOCK // 2 * chan_here)], 1)

    extent = own_cells(counts[...])
    place = lax.broadcasted_iota(jnp.int32, (1, 2 * BLOCK), 1)
    place += jnp.where(place < BLOCK, 2 * BLOCK * chan_here, BLOCK // 2 * chan_here)
    live = place < cells_ref[tile_here]
    scale = jnp.where(live, 1.6 / jnp.sqrt(extent), 0.0)
    rate = own_cells(rates[...])
    write_taps(extent, rate, scale, tap_ref, KMAX // 2 - pulses)
    taps = tap_ref[...]
    high = table[2 * points : 4 * points]
    low = table[4 * points : 6 * points]
    response = jnp.dot(high, taps, preferred_element_type=jnp.float32) + jnp.dot(
        low, taps, preferred_element_type=jnp.float32
    )
    turned[...] = response.T

    image = None
    for half in range(2):
        parts = []
        for group in (2 * half, 2 * half + 1):
            for at in range(4):
                source = 4 * group + at

                @pl.when(source != here)
                def _():
                    pltpu.make_async_remote_copy(
                        src_ref=packed.at[source // 2, source % 2],
                        dst_ref=columns.at[group, :, at],
                        send_sem=send_sems.at[0],
                        recv_sem=recv_sems.at[source],
                        device_id={"tile": source // 2, "chan": source % 2},
                        device_id_type=MESH,
                    ).wait_recv()

            whole = columns[group, :2].reshape(BLOCK, BLOCK).T
            folded = columns[group, 2].reshape(BLOCK // 2, BLOCK).astype(jnp.float32).T
            folded = jnp.concatenate([folded[: BLOCK // 2], folded[BLOCK // 2 :]], 1)
            parts.append(jnp.concatenate([whole, folded.astype(jnp.bfloat16)], 0))
        term = jnp.dot(
            jnp.concatenate(parts, 1),
            table[2 * half * BLOCK : 2 * (half + 1) * BLOCK],
            preferred_element_type=jnp.float32,
        )
        image = term if image is None else image + term
    slots = image.shape[0]
    real, imag = image[:, :points], image[:, points:]
    tap_real, tap_imag = turned[:slots, :points], turned[:slots, points:]
    product = jnp.concatenate(
        [real * tap_real - imag * tap_imag, real * tap_imag + imag * tap_real], 1
    ).astype(jnp.bfloat16)
    inverse = table[6 * points :]
    result = jnp.dot(
        product[:, :points], inverse[:, :points], preferred_element_type=jnp.float32
    ) + jnp.dot(product[:, points:], inverse[:, points:], preferred_element_type=jnp.float32)
    for part in range(2):
        lanes = slice(part * pulses, (part + 1) * pulses)
        out_ref[pl.ds(BLOCK * chan_here + part, BLOCK, stride=2), :] = result[:BLOCK, lanes]
        out_ref[pl.ds(2 * BLOCK * (1 - chan_here) + part, slots - BLOCK, stride=2), :] = result[
            BLOCK:, lanes
        ]
    for tile, chan in everyone:

        @pl.when(2 * tile + chan != here)
        def _():
            send(tile, chan).wait_send()


def focus_call(raw_echoes, range_taps, beam_weights, order, cells, counts, rates, half_cap):
    local, local_chans, _, cell_count = raw_echoes.shape
    tiles = cells.shape[0]
    pulses = tiles * local
    out_blocks = cell_count // BLOCK
    raw_echoes = raw_echoes.reshape(local, local_chans, 2, out_blocks, BLOCK)
    raw_echoes = raw_echoes.transpose(0, 1, 3, 2, 4).reshape(local, local_chans, -1, BLOCK)
    table = jnp.asarray(fourier_tables(pulses, local))
    counts, rates = counts[None], rates[None]
    arrays = [raw_echoes, range_taps, beam_weights, counts, rates, table]
    total = pltpu.VMEM((out_blocks, local, BLOCK), jnp.float32)
    result = pl.pallas_call(
        functools.partial(focus_kernel, half_cap),
        out_shape=pltpu.VMEM((2 * half_cap, pulses), jnp.float32),
        in_specs=[pl.BlockSpec(memory_space=pl.ANY)] * (2 + len(arrays)),
        out_specs=pl.BlockSpec(memory_space=pltpu.VMEM),
        scratch_shapes=[pltpu.SMEM(order.shape, order.dtype), pltpu.SMEM(cells.shape, cells.dtype)]
        + [pltpu.VMEM((2, local, local_chans, out_blocks, BLOCK), raw_echoes.dtype)]
        + [pltpu.VMEM(array.shape, array.dtype) for array in arrays[1:]]
        + [
            pltpu.VMEM((2 * BLOCK, 2 * BLOCK), jnp.bfloat16),
            pltpu.VMEM((local_chans, out_blocks + 4, local, 2 * BLOCK), jnp.bfloat16),
            pltpu.VMEM((local_chans, 2 * STEPS * BLOCK, 2 * BLOCK), jnp.bfloat16),
            total,
            total,
            pltpu.VMEM((tiles, 2, 3, local, BLOCK), jnp.bfloat16),
            pltpu.VMEM((tiles // 2, 3, 4, local, BLOCK), jnp.bfloat16),
            pltpu.VMEM((4 * pulses, 2 * BLOCK), jnp.bfloat16),
            pltpu.VMEM((2 * BLOCK, 4 * pulses), jnp.float32),
            pltpu.SemaphoreType.DMA((len(arrays) + 1,)),
            pltpu.SemaphoreType.DMA((local_chans,)),
            pltpu.SemaphoreType.DMA((2 * tiles,)),
            pltpu.SemaphoreType.DMA((2 * tiles,)),
        ],
        compiler_params=pltpu.CompilerParams(
            collective_id=0, has_side_effects=True, vmem_limit_bytes=56 << 20
        ),
    )(order, cells, *arrays)
    return result.reshape(half_cap, 2, pulses)


def on_device(
    raw_echoes, range_taps, beam_weights, channel_order, group_cells, tap_counts, chirp_rates
):
    tiles = group_cells.shape[0]
    local, _, _, cell_count = raw_echoes.shape
    average = cell_count // tiles
    half_cap = (average + average // 2) // lax.axis_size("chan")
    fits = average == 2 * BLOCK and lax.axis_size("chan") == 2 and local == 16 and tiles == 8
    if not fits or range_taps.shape[-1] != 4 * BLOCK:
        return generic_device(
            raw_echoes,
            range_taps,
            beam_weights,
            channel_order,
            group_cells,
            tap_counts,
            chirp_rates,
        )
    return focus_call(
        raw_echoes,
        range_taps,
        beam_weights,
        channel_order,
        group_cells,
        tap_counts,
        chirp_rates,
        half_cap,
    )


def solution(mesh):
    return jax.shard_map(
        on_device,
        mesh=mesh,
        in_specs=(P(("scene", "tile"), "chan", None, None), P(), P(), P(), P(), P(), P()),
        out_specs=P(("scene", "tile", "chan"), None, None),
        check_vma=False,
    )
```

```python
import functools

import jax
import jax.numpy as jnp
import numpy as np
from jax import lax
from jax.experimental import pallas as pl
from jax.experimental.pallas import tpu as pltpu
from jax.sharding import PartitionSpec as P

KMAX = 640


def toeplitz_rows(coeffs, block_len, span_len):
    leading = coeffs.shape[:-1]
    filler = jnp.zeros(leading + (span_len + 1 - coeffs.shape[-1],), coeffs.dtype)
    extended = jnp.concatenate([coeffs, filler], -1)
    repeated = jnp.tile(extended, (1,) * len(leading) + (block_len,))
    return repeated[..., : block_len * span_len].reshape(leading + (block_len, span_len))


def complex_matrix(toeplitz_pair):
    real_part = toeplitz_pair[..., 0, :, :]
    imag_part = toeplitz_pair[..., 1, :, :]
    from_real = jnp.stack([real_part, imag_part], -3)
    from_imag = jnp.stack([-imag_part, real_part], -3)
    return jnp.stack([from_real, from_imag], -4)


def block_windows(signal, block_len, lead_blocks, span_blocks, out_blocks):
    total_blocks = out_blocks + span_blocks - 1
    right_pad = total_blocks * block_len - lead_blocks * block_len - signal.shape[-1]
    padded = jnp.pad(signal, [(0, 0)] * (signal.ndim - 1) + [(lead_blocks * block_len, right_pad)])
    blocked = padded.reshape(signal.shape[:-1] + (total_blocks, block_len))
    return jnp.concatenate(
        [
            blocked[..., offset_block : offset_block + out_blocks, :]
            for offset_block in range(span_blocks)
        ],
        -1,
    )


def chirp_taps(counts, sweep_rates, longest):
    position = jnp.arange(longest, dtype=jnp.int32)[None, :]
    lengths = counts[:, None]
    shifted = position - (longest // 2 - lengths // 2)
    inside = (shifted >= 0) & (shifted < lengths)
    extent = lengths.astype(jnp.float32)
    located = shifted.astype(jnp.float32)
    centred = (located - 0.5 * (extent - 1.0)) / extent
    angles = jnp.pi * sweep_rates[:, None] * extent * centred * centred
    envelope = (
        (0.5 - 0.5 * jnp.cos(2.0 * jnp.pi * (located + 0.5) / extent)) * 1.6 / jnp.sqrt(extent)
    )
    envelope = jnp.where(inside, envelope, jnp.zeros_like(envelope))
    return jnp.stack([envelope * jnp.cos(angles), envelope * jnp.sin(angles)], 1)


def range_compress(echoes, filters):
    block_len = filters.shape[-1] // 2
    windows = block_windows(echoes, block_len, 1, 3, echoes.shape[-1] // block_len)
    matrices = complex_matrix(toeplitz_rows(filters, block_len, 3 * block_len))
    product = jnp.einsum(
        "pcanw,caeiw->pceni", windows, matrices, preferred_element_type=jnp.float32
    )
    return product.reshape(echoes.shape)


def azimuth_focus(columns, coeffs):
    block_len = coeffs.shape[-1] // 8
    pulses = columns.shape[-1]
    out_blocks = -(-pulses // block_len)
    windows = block_windows(columns, block_len, 4, 9, out_blocks)
    matrices = complex_matrix(toeplitz_rows(coeffs, block_len, 9 * block_len))
    product = jnp.einsum("sanw,saeiw->seni", windows, matrices, preferred_element_type=jnp.float32)
    return product.reshape(columns.shape[:-1] + (out_blocks * block_len,))[..., :pulses]


def owner_slots(signal, group_starts, group_sizes, offset, slot_width, margin):
    padded = jnp.pad(signal, [(0, 0)] * (signal.ndim - 1) + [(0, margin)])

    def one_group(start_cell, size_cells):
        window_cut = lax.dynamic_slice_in_dim(
            padded, start_cell + offset, slot_width, signal.ndim - 1
        )
        inside = jnp.arange(slot_width, dtype=jnp.int32) + offset < size_cells
        return jnp.where(inside, window_cut, jnp.zeros_like(window_cut))

    return jax.vmap(one_group)(group_starts, group_sizes)


def generic_device(
    raw_echoes, range_taps, beam_weights, channel_order, group_cells, tap_counts, chirp_rates
):
    local_chans = raw_echoes.shape[1]
    all_chans = range_taps.shape[0]
    first_slot = lax.axis_index("chan") * local_chans
    own_channels = lax.dynamic_slice_in_dim(channel_order, first_slot, local_chans)
    selector = (own_channels[:, None] == jnp.arange(all_chans, dtype=jnp.int32)[None, :]).astype(
        jnp.bfloat16
    )
    filters = jnp.dot(
        selector, range_taps.reshape(all_chans, -1), preferred_element_type=jnp.float32
    )
    filters = filters.astype(jnp.bfloat16).reshape(local_chans, 2, -1)
    weights = jnp.dot(
        selector, beam_weights.reshape(all_chans, -1), preferred_element_type=jnp.float32
    )
    weights = weights.reshape(local_chans, 2, -1)
    spectra = range_compress(raw_echoes, filters)
    real_sum = jnp.sum(spectra[:, :, 0] * weights[:, 0] - spectra[:, :, 1] * weights[:, 1], 1)
    imag_sum = jnp.sum(spectra[:, :, 0] * weights[:, 1] + spectra[:, :, 1] * weights[:, 0], 1)
    partial_value = jnp.stack([real_sum, imag_sum], 1)
    tile_count = group_cells.shape[0]
    cell_count = raw_echoes.shape[-1]
    average = cell_count // tile_count
    capacity = average + average // 2
    chan_ways = lax.axis_size("chan")
    half_cap = capacity // chan_ways
    group_starts = jnp.cumsum(group_cells) - group_cells
    chan_offset = lax.axis_index("chan") * half_cap
    summed = lax.psum(partial_value.astype(jnp.bfloat16), "chan")
    outgoing = owner_slots(summed, group_starts, group_cells, chan_offset, half_cap, capacity)
    outgoing = outgoing.transpose(0, 3, 2, 1)
    incoming = lax.all_to_all(outgoing, "tile", split_axis=0, concat_axis=3, tiled=True)
    columns = incoming[0]
    tile_here = lax.axis_index("tile")
    begin_cell = lax.dynamic_index_in_dim(group_starts, tile_here, keepdims=False)
    owned_cells = lax.dynamic_index_in_dim(group_cells, tile_here, keepdims=False)
    local_slot = chan_offset + jnp.arange(half_cap, dtype=jnp.int32)
    inside = local_slot < owned_cells
    count_table = jnp.pad(tap_counts, (0, capacity), mode="edge")
    rate_table = jnp.pad(chirp_rates, (0, capacity), mode="edge")
    count_here = lax.dynamic_slice_in_dim(count_table, begin_cell + chan_offset, half_cap)
    rate_here = lax.dynamic_slice_in_dim(rate_table, begin_cell + chan_offset, half_cap)
    taps_here = chirp_taps(count_here, rate_here, KMAX)
    taps_here = jnp.where(inside[:, None, None], taps_here, jnp.zeros_like(taps_here)).astype(
        jnp.bfloat16
    )
    return azimuth_focus(columns, taps_here)


MESH = pl.DeviceIdType.MESH
BLOCK = 128
STEPS = 5
SPAN = STEPS * BLOCK


def split_bf16(matrix):
    high = matrix.astype(jnp.bfloat16)
    low = (matrix - high.astype(np.float64)).astype(jnp.bfloat16)
    return np.stack([high, low])


def fourier_tables(pulses, local):
    points = 2 * pulses
    freq = np.arange(points)[:, None]
    unit = 2.0 * np.pi / points

    def rotation(index, sign):
        angle = unit * ((freq * index[None, :]) % points)
        return np.cos(angle), sign * np.sin(angle)

    cos_x, sin_x = rotation(np.arange(pulses), -1.0)
    forward = np.stack([np.concatenate([cos_x, sin_x]).T, np.concatenate([-sin_x, cos_x]).T])
    forward = forward.reshape(2, 2, -1, 1, local, 2 * points)
    forward = np.broadcast_to(forward, forward.shape[:3] + (2,) + forward.shape[4:])
    forward = forward.transpose(1, 0, 2, 3, 4, 5).reshape(-1, 2 * points)
    cos_h, sin_h = rotation(pulses - np.arange(points), -1.0)
    taps = np.block([[cos_h, -sin_h], [sin_h, cos_h]])
    cos_y, sin_y = rotation(np.arange(pulses), 1.0)
    inverse = np.block([[cos_y, sin_y], [-sin_y, cos_y]]) / points
    inverse = np.concatenate([inverse[:points], inverse[points:]], 1)
    table = np.concatenate([forward.astype(jnp.bfloat16), *split_bf16(taps)])
    return np.concatenate([table, inverse.astype(jnp.bfloat16)])


def even_series(square, terms):
    value = jnp.full_like(square, terms[-1])
    for term in reversed(terms[:-1]):
        value = value * square + term
    return value


COS_TERMS = [(-1.0) ** n * (2 * np.pi) ** (2 * n) / float(np.prod(np.arange(1, 2 * n + 1, dtype=np.float64))) for n in range(9)]
SIN_TERMS = [(-1.0) ** n * (2 * np.pi) ** (2 * n + 1) / float(np.prod(np.arange(1, 2 * n + 2, dtype=np.float64))) for n in range(9)]


def write_taps(extent, rate, scale, tap_ref, first_tap):
    rows = tap_ref.shape[0] // 2
    length = extent.astype(jnp.int32)
    start = KMAX // 2 - length // 2
    inverse = 1.0 / extent
    turn = 0.5 * rate * extent
    for at in range(0, rows, 32):
        tap = lax.broadcasted_iota(jnp.int32, (32, 2 * BLOCK), 0) + (first_tap + at)
        shifted = tap - start
        inside = (shifted >= 0) & (shifted < length)
        centred = (shifted.astype(jnp.float32) - 0.5 * (extent - 1.0)) * inverse
        square = centred * centred
        envelope = jnp.where(inside, scale * (0.5 + 0.5 * even_series(square, COS_TERMS)), 0.0)
        turns = turn * square
        turns = turns - jnp.floor(turns + 0.5)
        turn_square = turns * turns
        real = envelope * even_series(turn_square, COS_TERMS)
        imag = envelope * (turns * even_series(turn_square, SIN_TERMS))
        tap_ref[at : at + 32] = real.astype(jnp.bfloat16)
        tap_ref[rows + at : rows + at + 32] = imag.astype(jnp.bfloat16)


def focus_kernel(
    half_cap,
    order_hbm,
    cells_hbm,
    raw_ref,
    filter_ref,
    weight_ref,
    count_ref,
    rate_ref,
    table_ref,
    out_ref,
    order_ref,
    cells_ref,
    raw,
    filters,
    weights,
    counts,
    rates,
    table,
    mirror,
    blocks,
    matrices,
    real_sum,
    imag_sum,
    packed,
    columns,
    tap_ref,
    turned,
    load_sems,
    raw_sems,
    send_sem,
    recv_sems,
):
    tiles = packed.shape[0] // 2
    tile_here = lax.axis_index("tile")
    chan_here = lax.axis_index("chan")
    here = 2 * tile_here + chan_here
    local, local_chans, pieces, _ = raw.shape[1:]
    out_blocks = pieces
    pulses = tiles * local
    points = 2 * pulses
    def fetch(source, target, at):
        return pltpu.make_async_copy(source, target, load_sems.at[at])

    def fetch_raw(half, group):
        chans = pl.ds(2 * group, 2)
        return pltpu.make_async_copy(
            raw_ref.at[:, chans, pl.ds(half * pieces, pieces)],
            raw.at[half, :, chans],
            raw_sems.at[half * (local_chans // 2) + group],
        )

    get_filters = fetch(filter_ref, filters, 0)
    get_weights = fetch(weight_ref, weights, 1)
    late = [
        fetch(count_ref, counts, 2),
        fetch(rate_ref, rates, 3),
        fetch(table_ref, table, 4),
    ]
    get_order = fetch(order_hbm, order_ref, 5)
    get_cells = fetch(cells_hbm, cells_ref, 6)
    get_order.start()
    get_filters.start()
    for group in range(local_chans // 2):
        fetch_raw(0, group).start()
    get_weights.start()
    get_cells.start()
    for group in range(local_chans // 2):
        fetch_raw(1, group).start()
    for copy in late:
        copy.start()

    barrier = pltpu.get_barrier_semaphore()
    everyone = [(tile, chan) for tile in range(tiles) for chan in range(2)]
    for tile, chan in everyone:

        @pl.when(2 * tile + chan != here)
        def _():
            pl.semaphore_signal(
                barrier, inc=1, device_id={"tile": tile, "chan": chan}, device_id_type=MESH
            )

    edge = jnp.zeros((local_chans, 2, local, 2 * BLOCK), jnp.bfloat16)
    blocks[:, :2] = edge
    blocks[:, out_blocks + 2 :] = edge
    row = lax.broadcasted_iota(jnp.int32, (2 * BLOCK, 2 * BLOCK), 0)
    lane = lax.broadcasted_iota(jnp.int32, (2 * BLOCK, 2 * BLOCK), 1)
    mirror[...] = jnp.where(row + lane == 2 * BLOCK - 1, 1.0, 0.0).astype(jnp.bfloat16)
    get_order.wait()
    get_filters.wait()

    physical = [order_ref[chan_here * local_chans + chan] for chan in range(local_chans)]
    own = jnp.concatenate([filters[at].astype(jnp.float32) for at in physical], 0)
    own = own.astype(jnp.bfloat16)
    backward = jnp.concatenate(
        [
            jnp.dot(own[:, 2 * BLOCK :], mirror[...], preferred_element_type=jnp.float32),
            jnp.dot(own[:, : 2 * BLOCK], mirror[...], preferred_element_type=jnp.float32),
            jnp.zeros((2 * local_chans, BLOCK), jnp.float32),
        ],
        1,
    ).astype(jnp.bfloat16)
    def toeplitz(at):
        row = jnp.broadcast_to(backward[at : at + 1], (BLOCK, SPAN))
        return pltpu.roll(row, 1, 1, stride=1, stride_axis=0)

    def write_matrices(group):
        for chan in (2 * group, 2 * group + 1):
            real_rows = toeplitz(2 * chan)
            imag_rows = toeplitz(2 * chan + 1)
            for step in range(STEPS):
                at = slice((4 - step) * BLOCK, (5 - step) * BLOCK)
                real = real_rows[:, at]
                imag = imag_rows[:, at]
                upper = slice(2 * step * BLOCK, (2 * step + 1) * BLOCK)
                lower = slice((2 * step + 1) * BLOCK, (2 * step + 2) * BLOCK)
                matrices[chan, upper, :BLOCK] = real
                matrices[chan, upper, BLOCK:] = imag
                matrices[chan, lower, :BLOCK] = -imag
                matrices[chan, lower, BLOCK:] = real

    def spread_rows(half, group):
        fetch_raw(half, group).wait()
        for chan in (2 * group, 2 * group + 1):
            wide = jnp.swapaxes(raw[half, :, chan].astype(jnp.float32), 0, 1).astype(jnp.bfloat16)
            for block in range(pieces // 2):
                at = half * (pieces // 2) + block + 2
                blocks[chan, at, :, :BLOCK] = wide[2 * block]
                blocks[chan, at, :, BLOCK:] = wide[2 * block + 1]

    def compress(chan, first, last):
        total = None
        for step in range(STEPS):
            window = blocks[chan, first + step : last + step].reshape(-1, 2 * BLOCK)
            matrix = matrices[chan, 2 * step * BLOCK : 2 * (step + 1) * BLOCK]
            term = jnp.dot(window, matrix, preferred_element_type=jnp.float32)
            total = term if total is None else total + term
        return total

    def beamform(chan, first, last, total):
        own_weight = weights[physical[chan]].astype(jnp.float32)
        for block in range(first, last):
            cells = slice(block * BLOCK, (block + 1) * BLOCK)
            weight_real = own_weight[0:1, cells]
            weight_imag = own_weight[1:2, cells]
            real = total[(block - first) * local : (block - first + 1) * local, :BLOCK]
            imag = total[(block - first) * local : (block - first + 1) * local, BLOCK:]
            new_real = weight_real * real - weight_imag * imag
            new_imag = weight_imag * real + weight_real * imag
            if chan > 0:
                new_real += real_sum[block]
                new_imag += imag_sum[block]
            real_sum[block] = new_real
            imag_sum[block] = new_imag

    def phase(group, first, last):
        chans = (2 * group, 2 * group + 1)
        totals = [compress(chan, first, last) for chan in chans]
        for chan, total in zip(chans, totals):
            beamform(chan, first, last, total)

    is_left = lax.broadcasted_iota(jnp.int32, (local, BLOCK), 1) < BLOCK // 2

    def pack(tile, real, imag):
        def put(chan, at):
            cells = slice(at * BLOCK, (at + 1) * BLOCK)
            packed[2 * tile + chan, 0] = real[:, cells].astype(jnp.bfloat16)
            packed[2 * tile + chan, 1] = imag[:, cells].astype(jnp.bfloat16)

        put(0, 0)
        put(1, 2)
        half_real, half_imag = real[:, BLOCK : 2 * BLOCK], imag[:, BLOCK : 2 * BLOCK]
        packed[2 * tile, 2] = jnp.where(
            is_left, half_real, pltpu.roll(half_imag, BLOCK // 2, 1)
        ).astype(jnp.bfloat16)
        packed[2 * tile + 1, 2] = jnp.where(
            is_left, pltpu.roll(half_real, BLOCK // 2, 1), half_imag
        ).astype(jnp.bfloat16)

    half_here, place_here = here // tiles, lax.rem(here, tiles)

    def send(peer):
        return pltpu.make_async_remote_copy(
            src_ref=packed.at[peer],
            dst_ref=columns.at[half_here, :, place_here],
            send_sem=send_sem,
            recv_sem=recv_sems.at[half_here],
            device_id={"tile": peer // 2, "chan": peer % 2},
            device_id_type=MESH,
        )

    def keep(peer):
        return pltpu.make_async_copy(
            packed.at[peer], columns.at[half_here, :, place_here], recv_sems.at[half_here]
        )

    def deliver(pair):
        first = cells_ref[2 * pair]
        real = jnp.concatenate([real_sum[4 * pair + at] for at in range(4)], 1)
        imag = jnp.concatenate([imag_sum[4 * pair + at] for at in range(4)], 1)
        pack(2 * pair, real, imag)
        both = pltpu.roll(jnp.concatenate([real, imag], 0), 4 * BLOCK - first, 1)
        pack(2 * pair + 1, both[:local], both[local:])
        if pair == 0:
            pl.semaphore_wait(barrier, 2 * tiles - 1)
        for peer in range(4 * pair, 4 * pair + 4):

            @pl.when(peer != here)
            def _():
                send(peer).start()

            @pl.when(peer == here)
            def _():
                keep(peer).start()

    groups = local_chans // 2
    write_matrices(0)
    get_weights.wait()
    for group in range(groups):
        spread_rows(0, group)
        if group + 1 < groups:
            write_matrices(group + 1)
        phase(group, 0, 4)

    def second_phase():
        for group in range(groups):
            spread_rows(1, group)
        for group in range(groups):
            phase(group, 4, out_blocks)

    get_cells.wait()
    early = tile_here < tiles // 2
    pl.when(early)(second_phase)
    deliver(0)
    pl.when(jnp.logical_not(early))(second_phase)
    for pair in range(1, tiles // 2):
        deliver(pair)
    for copy in late:
        copy.wait()
    begin = 0
    for tile in range(tiles):
        begin += jnp.where(tile < tile_here, cells_ref[tile], 0)
    cell_count = counts.shape[1]

    def own_cells(table):
        wide = jnp.broadcast_to(table.astype(jnp.float32), (8, cell_count))

        def cut(at):
            shift = lax.rem(2 * cell_count - begin - at, cell_count)
            return pltpu.roll(wide, shift, 1)[0:1, :BLOCK]

        return jnp.concatenate([cut(2 * BLOCK * chan_here), cut(BLOCK + BLOCK // 2 * chan_here)], 1)

    extent = own_cells(counts[...])
    place = lax.broadcasted_iota(jnp.int32, (1, 2 * BLOCK), 1)
    place += jnp.where(place < BLOCK, 2 * BLOCK * chan_here, BLOCK // 2 * chan_here)
    live = place < cells_ref[tile_here]
    scale = jnp.where(live, 1.6 / jnp.sqrt(extent), 0.0)
    rate = own_cells(rates[...])
    write_taps(extent, rate, scale, tap_ref, KMAX // 2 - pulses)
    taps = tap_ref[...]
    high = table[2 * points : 4 * points]
    low = table[4 * points : 6 * points]
    response = jnp.dot(high, taps, preferred_element_type=jnp.float32) + jnp.dot(
        low, taps, preferred_element_type=jnp.float32
    )
    turned[...] = response.T

    image = None
    for half in range(2):
        pltpu.make_async_copy(columns.at[half], columns.at[half], recv_sems.at[half]).wait()
        pieces = [columns[half, at].reshape(BLOCK, BLOCK).T for at in range(3)]
        signal = jnp.concatenate(
            [
                jnp.concatenate(pieces[:2], 1),
                jnp.concatenate([pieces[2][: BLOCK // 2], pieces[2][BLOCK // 2 :]], 1),
            ],
            0,
        )
        term = jnp.dot(
            signal,
            table[2 * half * BLOCK : 2 * (half + 1) * BLOCK],
            preferred_element_type=jnp.float32,
        )
        image = term if image is None else image + term
    slots = image.shape[0]
    real, imag = image[:, :points], image[:, points:]
    tap_real, tap_imag = turned[:slots, :points], turned[:slots, points:]
    product = jnp.concatenate(
        [real * tap_real - imag * tap_imag, real * tap_imag + imag * tap_real], 1
    ).astype(jnp.bfloat16)
    inverse = table[6 * points :]
    result = jnp.dot(
        product[:, :points], inverse[:, :points], preferred_element_type=jnp.float32
    ) + jnp.dot(product[:, points:], inverse[:, points:], preferred_element_type=jnp.float32)
    for part in range(2):
        lanes = slice(part * pulses, (part + 1) * pulses)
        out_ref[pl.ds(BLOCK * chan_here + part, BLOCK, stride=2), :] = result[:BLOCK, lanes]
        out_ref[pl.ds(2 * BLOCK * (1 - chan_here) + part, slots - BLOCK, stride=2), :] = result[
            BLOCK:, lanes
        ]
    sent = packed.at[pl.ds(0, 2 * tiles - 1)]
    pltpu.make_async_copy(sent, sent, send_sem).wait()


def focus_call(raw_echoes, range_taps, beam_weights, order, cells, counts, rates, half_cap):
    local, local_chans, _, cell_count = raw_echoes.shape
    tiles = cells.shape[0]
    pulses = tiles * local
    out_blocks = cell_count // BLOCK
    raw_echoes = raw_echoes.reshape(local, local_chans, 2, out_blocks, BLOCK)
    raw_echoes = raw_echoes.transpose(0, 1, 3, 2, 4).reshape(local, local_chans, -1, BLOCK)
    table = jnp.asarray(fourier_tables(pulses, local))
    counts, rates = counts[None], rates[None]
    arrays = [raw_echoes, range_taps, beam_weights, counts, rates, table]
    total = pltpu.VMEM((out_blocks, local, BLOCK), jnp.float32)
    result = pl.pallas_call(
        functools.partial(focus_kernel, half_cap),
        out_shape=pltpu.VMEM((2 * half_cap, pulses), jnp.float32),
        in_specs=[pl.BlockSpec(memory_space=pl.ANY)] * (2 + len(arrays)),
        out_specs=pl.BlockSpec(memory_space=pltpu.VMEM),
        scratch_shapes=[pltpu.SMEM(order.shape, order.dtype), pltpu.SMEM(cells.shape, cells.dtype)]
        + [pltpu.VMEM((2, local, local_chans, out_blocks, BLOCK), raw_echoes.dtype)]
        + [pltpu.VMEM(array.shape, array.dtype) for array in arrays[1:]]
        + [
            pltpu.VMEM((2 * BLOCK, 2 * BLOCK), jnp.bfloat16),
            pltpu.VMEM((local_chans, out_blocks + 4, local, 2 * BLOCK), jnp.bfloat16),
            pltpu.VMEM((local_chans, 2 * STEPS * BLOCK, 2 * BLOCK), jnp.bfloat16),
            total,
            total,
            pltpu.VMEM((2 * tiles, 3, local, BLOCK), jnp.bfloat16),
            pltpu.VMEM((2, 3, tiles, local, BLOCK), jnp.bfloat16),
            pltpu.VMEM((4 * pulses, 2 * BLOCK), jnp.bfloat16),
            pltpu.VMEM((2 * BLOCK, 4 * pulses), jnp.float32),
            pltpu.SemaphoreType.DMA((len(arrays) + 1,)),
            pltpu.SemaphoreType.DMA((local_chans,)),
            pltpu.SemaphoreType.DMA(()),
            pltpu.SemaphoreType.DMA((2,)),
        ],
        compiler_params=pltpu.CompilerParams(
            collective_id=0, has_side_effects=True, vmem_limit_bytes=56 << 20
        ),
    )(order, cells, *arrays)
    return result.reshape(half_cap, 2, pulses)


def on_device(
    raw_echoes, range_taps, beam_weights, channel_order, group_cells, tap_counts, chirp_rates
):
    tiles = group_cells.shape[0]
    local, _, _, cell_count = raw_echoes.shape
    average = cell_count // tiles
    half_cap = (average + average // 2) // lax.axis_size("chan")
    fits = average == 2 * BLOCK and lax.axis_size("chan") == 2 and local == 16 and tiles == 8
    if not fits or range_taps.shape[-1] != 4 * BLOCK:
        return generic_device(
            raw_echoes,
            range_taps,
            beam_weights,
            channel_order,
            group_cells,
            tap_counts,
            chirp_rates,
        )
    return focus_call(
        raw_echoes,
        range_taps,
        beam_weights,
        channel_order,
        group_cells,
        tap_counts,
        chirp_rates,
        half_cap,
    )


def solution(mesh):
    return jax.shard_map(
        on_device,
        mesh=mesh,
        in_specs=(P(("scene", "tile"), "chan", None, None), P(), P(), P(), P(), P(), P()),
        out_specs=P(("scene", "tile", "chan"), None, None),
        check_vma=False,
    )
```

```python
import functools

import jax
import jax.numpy as jnp
import numpy as np
from jax import lax
from jax.experimental import pallas as pl
from jax.experimental.pallas import tpu as pltpu
from jax.sharding import PartitionSpec as P

KMAX = 640


def toeplitz_rows(coeffs, block_len, span_len):
    leading = coeffs.shape[:-1]
    filler = jnp.zeros(leading + (span_len + 1 - coeffs.shape[-1],), coeffs.dtype)
    extended = jnp.concatenate([coeffs, filler], -1)
    repeated = jnp.tile(extended, (1,) * len(leading) + (block_len,))
    return repeated[..., : block_len * span_len].reshape(leading + (block_len, span_len))


def complex_matrix(toeplitz_pair):
    real_part = toeplitz_pair[..., 0, :, :]
    imag_part = toeplitz_pair[..., 1, :, :]
    from_real = jnp.stack([real_part, imag_part], -3)
    from_imag = jnp.stack([-imag_part, real_part], -3)
    return jnp.stack([from_real, from_imag], -4)


def block_windows(signal, block_len, lead_blocks, span_blocks, out_blocks):
    total_blocks = out_blocks + span_blocks - 1
    right_pad = total_blocks * block_len - lead_blocks * block_len - signal.shape[-1]
    padded = jnp.pad(signal, [(0, 0)] * (signal.ndim - 1) + [(lead_blocks * block_len, right_pad)])
    blocked = padded.reshape(signal.shape[:-1] + (total_blocks, block_len))
    return jnp.concatenate(
        [
            blocked[..., offset_block : offset_block + out_blocks, :]
            for offset_block in range(span_blocks)
        ],
        -1,
    )


def chirp_taps(counts, sweep_rates, longest):
    position = jnp.arange(longest, dtype=jnp.int32)[None, :]
    lengths = counts[:, None]
    shifted = position - (longest // 2 - lengths // 2)
    inside = (shifted >= 0) & (shifted < lengths)
    extent = lengths.astype(jnp.float32)
    located = shifted.astype(jnp.float32)
    centred = (located - 0.5 * (extent - 1.0)) / extent
    angles = jnp.pi * sweep_rates[:, None] * extent * centred * centred
    envelope = (
        (0.5 - 0.5 * jnp.cos(2.0 * jnp.pi * (located + 0.5) / extent)) * 1.6 / jnp.sqrt(extent)
    )
    envelope = jnp.where(inside, envelope, jnp.zeros_like(envelope))
    return jnp.stack([envelope * jnp.cos(angles), envelope * jnp.sin(angles)], 1)


def range_compress(echoes, filters):
    block_len = filters.shape[-1] // 2
    windows = block_windows(echoes, block_len, 1, 3, echoes.shape[-1] // block_len)
    matrices = complex_matrix(toeplitz_rows(filters, block_len, 3 * block_len))
    product = jnp.einsum(
        "pcanw,caeiw->pceni", windows, matrices, preferred_element_type=jnp.float32
    )
    return product.reshape(echoes.shape)


def azimuth_focus(columns, coeffs):
    block_len = coeffs.shape[-1] // 8
    pulses = columns.shape[-1]
    out_blocks = -(-pulses // block_len)
    windows = block_windows(columns, block_len, 4, 9, out_blocks)
    matrices = complex_matrix(toeplitz_rows(coeffs, block_len, 9 * block_len))
    product = jnp.einsum("sanw,saeiw->seni", windows, matrices, preferred_element_type=jnp.float32)
    return product.reshape(columns.shape[:-1] + (out_blocks * block_len,))[..., :pulses]


def owner_slots(signal, group_starts, group_sizes, offset, slot_width, margin):
    padded = jnp.pad(signal, [(0, 0)] * (signal.ndim - 1) + [(0, margin)])

    def one_group(start_cell, size_cells):
        window_cut = lax.dynamic_slice_in_dim(
            padded, start_cell + offset, slot_width, signal.ndim - 1
        )
        inside = jnp.arange(slot_width, dtype=jnp.int32) + offset < size_cells
        return jnp.where(inside, window_cut, jnp.zeros_like(window_cut))

    return jax.vmap(one_group)(group_starts, group_sizes)


def generic_device(
    raw_echoes, range_taps, beam_weights, channel_order, group_cells, tap_counts, chirp_rates
):
    local_chans = raw_echoes.shape[1]
    all_chans = range_taps.shape[0]
    first_slot = lax.axis_index("chan") * local_chans
    own_channels = lax.dynamic_slice_in_dim(channel_order, first_slot, local_chans)
    selector = (own_channels[:, None] == jnp.arange(all_chans, dtype=jnp.int32)[None, :]).astype(
        jnp.bfloat16
    )
    filters = jnp.dot(
        selector, range_taps.reshape(all_chans, -1), preferred_element_type=jnp.float32
    )
    filters = filters.astype(jnp.bfloat16).reshape(local_chans, 2, -1)
    weights = jnp.dot(
        selector, beam_weights.reshape(all_chans, -1), preferred_element_type=jnp.float32
    )
    weights = weights.reshape(local_chans, 2, -1)
    spectra = range_compress(raw_echoes, filters)
    real_sum = jnp.sum(spectra[:, :, 0] * weights[:, 0] - spectra[:, :, 1] * weights[:, 1], 1)
    imag_sum = jnp.sum(spectra[:, :, 0] * weights[:, 1] + spectra[:, :, 1] * weights[:, 0], 1)
    partial_value = jnp.stack([real_sum, imag_sum], 1)
    tile_count = group_cells.shape[0]
    cell_count = raw_echoes.shape[-1]
    average = cell_count // tile_count
    capacity = average + average // 2
    chan_ways = lax.axis_size("chan")
    half_cap = capacity // chan_ways
    group_starts = jnp.cumsum(group_cells) - group_cells
    chan_offset = lax.axis_index("chan") * half_cap
    summed = lax.psum(partial_value.astype(jnp.bfloat16), "chan")
    outgoing = owner_slots(summed, group_starts, group_cells, chan_offset, half_cap, capacity)
    outgoing = outgoing.transpose(0, 3, 2, 1)
    incoming = lax.all_to_all(outgoing, "tile", split_axis=0, concat_axis=3, tiled=True)
    columns = incoming[0]
    tile_here = lax.axis_index("tile")
    begin_cell = lax.dynamic_index_in_dim(group_starts, tile_here, keepdims=False)
    owned_cells = lax.dynamic_index_in_dim(group_cells, tile_here, keepdims=False)
    local_slot = chan_offset + jnp.arange(half_cap, dtype=jnp.int32)
    inside = local_slot < owned_cells
    count_table = jnp.pad(tap_counts, (0, capacity), mode="edge")
    rate_table = jnp.pad(chirp_rates, (0, capacity), mode="edge")
    count_here = lax.dynamic_slice_in_dim(count_table, begin_cell + chan_offset, half_cap)
    rate_here = lax.dynamic_slice_in_dim(rate_table, begin_cell + chan_offset, half_cap)
    taps_here = chirp_taps(count_here, rate_here, KMAX)
    taps_here = jnp.where(inside[:, None, None], taps_here, jnp.zeros_like(taps_here)).astype(
        jnp.bfloat16
    )
    return azimuth_focus(columns, taps_here)


MESH = pl.DeviceIdType.MESH
BLOCK = 128
STEPS = 5
SPAN = STEPS * BLOCK


def split_bf16(matrix):
    high = matrix.astype(jnp.bfloat16)
    low = (matrix - high.astype(np.float64)).astype(jnp.bfloat16)
    return np.stack([high, low])


def fourier_tables(pulses, local):
    points = 2 * pulses
    freq = np.arange(points)[:, None]
    unit = 2.0 * np.pi / points

    def rotation(index, sign):
        angle = unit * ((freq * index[None, :]) % points)
        return np.cos(angle), sign * np.sin(angle)

    cos_x, sin_x = rotation(np.arange(pulses), -1.0)
    forward = np.stack([np.concatenate([cos_x, sin_x]).T, np.concatenate([-sin_x, cos_x]).T])
    forward = forward.reshape(2, 2, -1, 1, local, 2 * points)
    forward = np.broadcast_to(forward, forward.shape[:3] + (2,) + forward.shape[4:])
    forward = forward.transpose(1, 0, 2, 3, 4, 5).reshape(-1, 2 * points)
    cos_h, sin_h = rotation(pulses - np.arange(points), -1.0)
    taps = np.block([[cos_h, -sin_h], [sin_h, cos_h]])
    cos_y, sin_y = rotation(np.arange(pulses), 1.0)
    inverse = np.block([[cos_y, sin_y], [-sin_y, cos_y]]) / points
    inverse = np.concatenate([inverse[:points], inverse[points:]], 1)
    table = np.concatenate([forward.astype(jnp.bfloat16), *split_bf16(taps)])
    return np.concatenate([table, inverse.astype(jnp.bfloat16)])


def even_series(square, terms):
    value = jnp.full_like(square, terms[-1])
    for term in reversed(terms[:-1]):
        value = value * square + term
    return value


COS_TERMS = [(-1.0) ** n * (2 * np.pi) ** (2 * n) / float(np.prod(np.arange(1, 2 * n + 1, dtype=np.float64))) for n in range(9)]
SIN_TERMS = [(-1.0) ** n * (2 * np.pi) ** (2 * n + 1) / float(np.prod(np.arange(1, 2 * n + 2, dtype=np.float64))) for n in range(9)]


def write_taps(extent, rate, scale, tap_ref, first_tap):
    rows = tap_ref.shape[0] // 2
    length = extent.astype(jnp.int32)
    start = KMAX // 2 - length // 2
    inverse = 1.0 / extent
    turn = 0.5 * rate * extent
    for at in range(0, rows, 32):
        tap = lax.broadcasted_iota(jnp.int32, (32, 2 * BLOCK), 0) + (first_tap + at)
        shifted = tap - start
        inside = (shifted >= 0) & (shifted < length)
        centred = (shifted.astype(jnp.float32) - 0.5 * (extent - 1.0)) * inverse
        square = centred * centred
        envelope = jnp.where(inside, scale * (0.5 + 0.5 * even_series(square, COS_TERMS)), 0.0)
        turns = turn * square
        turns = turns - jnp.floor(turns + 0.5)
        turn_square = turns * turns
        real = envelope * even_series(turn_square, COS_TERMS)
        imag = envelope * (turns * even_series(turn_square, SIN_TERMS))
        tap_ref[at : at + 32] = real.astype(jnp.bfloat16)
        tap_ref[rows + at : rows + at + 32] = imag.astype(jnp.bfloat16)


def focus_kernel(
    half_cap,
    order_hbm,
    cells_hbm,
    raw_ref,
    filter_ref,
    weight_ref,
    count_ref,
    rate_ref,
    table_ref,
    out_ref,
    order_ref,
    cells_ref,
    raw,
    filters,
    weights,
    counts,
    rates,
    table,
    mirror,
    blocks,
    matrices,
    real_sum,
    imag_sum,
    packed,
    columns,
    tap_ref,
    turned,
    load_sems,
    raw_sems,
    send_sem,
    recv_sems,
):
    tiles = packed.shape[0] // 2
    tile_here = lax.axis_index("tile")
    chan_here = lax.axis_index("chan")
    here = 2 * tile_here + chan_here
    local, local_chans, pieces, _ = raw.shape[1:]
    out_blocks = pieces
    pulses = tiles * local
    points = 2 * pulses
    def fetch(source, target, at):
        return pltpu.make_async_copy(source, target, load_sems.at[at])

    def fetch_raw(half, group):
        chans = pl.ds(2 * group, 2)
        return pltpu.make_async_copy(
            raw_ref.at[:, chans, pl.ds(half * pieces, pieces)],
            raw.at[half, :, chans],
            raw_sems.at[half * (local_chans // 2) + group],
        )

    get_filters = fetch(filter_ref, filters, 0)
    get_weights = fetch(weight_ref, weights, 1)
    late = [
        fetch(count_ref, counts, 2),
        fetch(rate_ref, rates, 3),
        fetch(table_ref, table, 4),
    ]
    get_order = fetch(order_hbm, order_ref, 5)
    get_cells = fetch(cells_hbm, cells_ref, 6)
    get_order.start()
    get_filters.start()
    for group in range(local_chans // 2):
        fetch_raw(0, group).start()
    get_weights.start()
    get_cells.start()
    for group in range(local_chans // 2):
        fetch_raw(1, group).start()
    for copy in late:
        copy.start()

    barrier = pltpu.get_barrier_semaphore()
    everyone = [(tile, chan) for tile in range(tiles) for chan in range(2)]
    for tile, chan in everyone:

        @pl.when(2 * tile + chan != here)
        def _():
            pl.semaphore_signal(
                barrier, inc=1, device_id={"tile": tile, "chan": chan}, device_id_type=MESH
            )

    edge = jnp.zeros((local_chans, 2, 2, local, BLOCK), jnp.bfloat16)
    blocks[:, :, :2] = edge
    blocks[:, :, out_blocks + 2 :] = edge
    row = lax.broadcasted_iota(jnp.int32, (2 * BLOCK, 2 * BLOCK), 0)
    lane = lax.broadcasted_iota(jnp.int32, (2 * BLOCK, 2 * BLOCK), 1)
    mirror[...] = jnp.where(row + lane == 2 * BLOCK - 1, 1.0, 0.0).astype(jnp.bfloat16)
    get_order.wait()
    get_filters.wait()

    physical = [order_ref[chan_here * local_chans + chan] for chan in range(local_chans)]
    own = jnp.concatenate([filters[at].astype(jnp.float32) for at in physical], 0)
    own = own.astype(jnp.bfloat16)
    backward = jnp.concatenate(
        [
            jnp.dot(own[:, 2 * BLOCK :], mirror[...], preferred_element_type=jnp.float32),
            jnp.dot(own[:, : 2 * BLOCK], mirror[...], preferred_element_type=jnp.float32),
            jnp.zeros((2 * local_chans, BLOCK), jnp.float32),
        ],
        1,
    ).astype(jnp.bfloat16)
    def toeplitz(at):
        row = jnp.broadcast_to(backward[at : at + 1], (BLOCK, SPAN))
        return pltpu.roll(row, 1, 1, stride=1, stride_axis=0)

    def write_matrices(group):
        for chan in (2 * group, 2 * group + 1):
            real_rows = toeplitz(2 * chan)
            imag_rows = toeplitz(2 * chan + 1)
            for step in range(STEPS):
                at = slice((4 - step) * BLOCK, (5 - step) * BLOCK)
                matrices[chan, step, 0] = real_rows[:, at]
                matrices[chan, step, 1] = imag_rows[:, at]

    def spread_rows(half, group):
        fetch_raw(half, group).wait()
        for chan in (2 * group, 2 * group + 1):
            wide = jnp.swapaxes(raw[half, :, chan].astype(jnp.float32), 0, 1).astype(jnp.bfloat16)
            for block in range(pieces // 2):
                at = half * (pieces // 2) + block + 2
                blocks[chan, 0, at] = wide[2 * block]
                blocks[chan, 1, at] = wide[2 * block + 1]

    def compress(chan, first, last):
        total = None
        for step in range(STEPS):
            window = jnp.concatenate(
                [
                    blocks[chan, part, first + step : last + step].reshape(-1, BLOCK)
                    for part in range(2)
                ],
                1,
            )
            real, imag = matrices[chan, step, 0], matrices[chan, step, 1]
            matrix = jnp.concatenate(
                [jnp.concatenate([real, imag], 1), jnp.concatenate([-imag, real], 1)], 0
            )
            term = jnp.dot(window, matrix, preferred_element_type=jnp.float32)
            total = term if total is None else total + term
        return total

    def beamform(chan, first, last, total):
        own_weight = weights[physical[chan]].astype(jnp.float32)
        for block in range(first, last):
            cells = slice(block * BLOCK, (block + 1) * BLOCK)
            weight_real = own_weight[0:1, cells]
            weight_imag = own_weight[1:2, cells]
            real = total[(block - first) * local : (block - first + 1) * local, :BLOCK]
            imag = total[(block - first) * local : (block - first + 1) * local, BLOCK:]
            new_real = weight_real * real - weight_imag * imag
            new_imag = weight_imag * real + weight_real * imag
            if chan > 0:
                new_real += real_sum[block]
                new_imag += imag_sum[block]
            real_sum[block] = new_real
            imag_sum[block] = new_imag

    def phase(group, first, last):
        chans = (2 * group, 2 * group + 1)
        totals = [compress(chan, first, last) for chan in chans]
        for chan, total in zip(chans, totals):
            beamform(chan, first, last, total)

    is_left = lax.broadcasted_iota(jnp.int32, (local, BLOCK), 1) < BLOCK // 2

    def pack(tile, real, imag):
        def put(chan, at):
            cells = slice(at * BLOCK, (at + 1) * BLOCK)
            packed[2 * tile + chan, 0] = real[:, cells].astype(jnp.bfloat16)
            packed[2 * tile + chan, 1] = imag[:, cells].astype(jnp.bfloat16)

        put(0, 0)
        put(1, 2)
        half_real, half_imag = real[:, BLOCK : 2 * BLOCK], imag[:, BLOCK : 2 * BLOCK]
        packed[2 * tile, 2] = jnp.where(
            is_left, half_real, pltpu.roll(half_imag, BLOCK // 2, 1)
        ).astype(jnp.bfloat16)
        packed[2 * tile + 1, 2] = jnp.where(
            is_left, pltpu.roll(half_real, BLOCK // 2, 1), half_imag
        ).astype(jnp.bfloat16)

    half_here, place_here = here // tiles, lax.rem(here, tiles)

    def send(peer):
        return pltpu.make_async_remote_copy(
            src_ref=packed.at[peer],
            dst_ref=columns.at[half_here, :, place_here],
            send_sem=send_sem,
            recv_sem=recv_sems.at[half_here],
            device_id={"tile": peer // 2, "chan": peer % 2},
            device_id_type=MESH,
        )

    def keep(peer):
        return pltpu.make_async_copy(
            packed.at[peer], columns.at[half_here, :, place_here], recv_sems.at[half_here]
        )

    def deliver(tile):
        pair = tile // 2
        parts = range(3 if tile == 0 else 4)
        real = jnp.concatenate([real_sum[4 * pair + at] for at in parts], 1)
        imag = jnp.concatenate([imag_sum[4 * pair + at] for at in parts], 1)
        if tile % 2 == 1:
            both = jnp.concatenate([real, imag], 0)
            both = pltpu.roll(both, 4 * BLOCK - cells_ref[2 * pair], 1)
            real, imag = both[:local], both[local:]
        pack(tile, real, imag)
        if tile == 0:
            pl.semaphore_wait(barrier, 2 * tiles - 1)
        for peer in (2 * tile, 2 * tile + 1):

            @pl.when(peer != here)
            def _():
                send(peer).start()

            @pl.when(peer == here)
            def _():
                keep(peer).start()

    groups = local_chans // 2
    write_matrices(0)
    get_weights.wait()
    for group in range(groups):
        spread_rows(0, group)
        if group + 1 < groups:
            write_matrices(group + 1)
        phase(group, 0, 3)

    def second_phase():
        for group in range(groups):
            spread_rows(1, group)
        for group in range(groups):
            phase(group, 3, out_blocks)

    get_cells.wait()
    early = tile_here < tiles // 2
    pl.when(early)(second_phase)
    deliver(0)
    pl.when(jnp.logical_not(early))(second_phase)
    for tile in range(1, tiles):
        deliver(tile)
    for copy in late:
        copy.wait()
    begin = 0
    for tile in range(tiles):
        begin += jnp.where(tile < tile_here, cells_ref[tile], 0)
    cell_count = counts.shape[1]

    def own_cells(table):
        wide = jnp.broadcast_to(table.astype(jnp.float32), (8, cell_count))

        def cut(at):
            shift = lax.rem(2 * cell_count - begin - at, cell_count)
            return pltpu.roll(wide, shift, 1)[0:1, :BLOCK]

        return jnp.concatenate([cut(2 * BLOCK * chan_here), cut(BLOCK + BLOCK // 2 * chan_here)], 1)

    extent = own_cells(counts[...])
    place = lax.broadcasted_iota(jnp.int32, (1, 2 * BLOCK), 1)
    place += jnp.where(place < BLOCK, 2 * BLOCK * chan_here, BLOCK // 2 * chan_here)
    live = place < cells_ref[tile_here]
    scale = jnp.where(live, 1.6 / jnp.sqrt(extent), 0.0)
    rate = own_cells(rates[...])
    write_taps(extent, rate, scale, tap_ref, KMAX // 2 - pulses)
    taps = tap_ref[...]
    high = table[2 * points : 4 * points]
    low = table[4 * points : 6 * points]
    response = jnp.dot(high, taps, preferred_element_type=jnp.float32) + jnp.dot(
        low, taps, preferred_element_type=jnp.float32
    )
    turned[...] = response.T

    image = None
    for half in range(2):
        pltpu.make_async_copy(columns.at[half], columns.at[half], recv_sems.at[half]).wait()
        pieces = [columns[half, at].reshape(BLOCK, BLOCK).T for at in range(3)]
        signal = jnp.concatenate(
            [
                jnp.concatenate(pieces[:2], 1),
                jnp.concatenate([pieces[2][: BLOCK // 2], pieces[2][BLOCK // 2 :]], 1),
            ],
            0,
        )
        term = jnp.dot(
            signal,
            table[2 * half * BLOCK : 2 * (half + 1) * BLOCK],
            preferred_element_type=jnp.float32,
        )
        image = term if image is None else image + term
    slots = image.shape[0]
    real, imag = image[:, :points], image[:, points:]
    tap_real, tap_imag = turned[:slots, :points], turned[:slots, points:]
    product = jnp.concatenate(
        [real * tap_real - imag * tap_imag, real * tap_imag + imag * tap_real], 1
    ).astype(jnp.bfloat16)
    inverse = table[6 * points :]
    result = jnp.dot(
        product[:, :points], inverse[:, :points], preferred_element_type=jnp.float32
    ) + jnp.dot(product[:, points:], inverse[:, points:], preferred_element_type=jnp.float32)
    for part in range(2):
        lanes = slice(part * pulses, (part + 1) * pulses)
        out_ref[pl.ds(BLOCK * chan_here + part, BLOCK, stride=2), :] = result[:BLOCK, lanes]
        out_ref[pl.ds(2 * BLOCK * (1 - chan_here) + part, slots - BLOCK, stride=2), :] = result[
            BLOCK:, lanes
        ]
    sent = packed.at[pl.ds(0, 2 * tiles - 1)]
    pltpu.make_async_copy(sent, sent, send_sem).wait()


def focus_call(raw_echoes, range_taps, beam_weights, order, cells, counts, rates, half_cap):
    local, local_chans, _, cell_count = raw_echoes.shape
    tiles = cells.shape[0]
    pulses = tiles * local
    out_blocks = cell_count // BLOCK
    raw_echoes = raw_echoes.reshape(local, local_chans, 2, out_blocks, BLOCK)
    raw_echoes = raw_echoes.transpose(0, 1, 3, 2, 4).reshape(local, local_chans, -1, BLOCK)
    table = jnp.asarray(fourier_tables(pulses, local))
    counts, rates = counts[None], rates[None]
    arrays = [raw_echoes, range_taps, beam_weights, counts, rates, table]
    total = pltpu.VMEM((out_blocks, local, BLOCK), jnp.float32)
    result = pl.pallas_call(
        functools.partial(focus_kernel, half_cap),
        out_shape=pltpu.VMEM((2 * half_cap, pulses), jnp.float32),
        in_specs=[pl.BlockSpec(memory_space=pl.ANY)] * (2 + len(arrays)),
        out_specs=pl.BlockSpec(memory_space=pltpu.VMEM),
        scratch_shapes=[pltpu.SMEM(order.shape, order.dtype), pltpu.SMEM(cells.shape, cells.dtype)]
        + [pltpu.VMEM((2, local, local_chans, out_blocks, BLOCK), raw_echoes.dtype)]
        + [pltpu.VMEM(array.shape, array.dtype) for array in arrays[1:]]
        + [
            pltpu.VMEM((2 * BLOCK, 2 * BLOCK), jnp.bfloat16),
            pltpu.VMEM((local_chans, 2, out_blocks + 4, local, BLOCK), jnp.bfloat16),
            pltpu.VMEM((local_chans, STEPS, 2, BLOCK, BLOCK), jnp.bfloat16),
            total,
            total,
            pltpu.VMEM((2 * tiles, 3, local, BLOCK), jnp.bfloat16),
            pltpu.VMEM((2, 3, tiles, local, BLOCK), jnp.bfloat16),
            pltpu.VMEM((4 * pulses, 2 * BLOCK), jnp.bfloat16),
            pltpu.VMEM((2 * BLOCK, 4 * pulses), jnp.float32),
            pltpu.SemaphoreType.DMA((len(arrays) + 1,)),
            pltpu.SemaphoreType.DMA((local_chans,)),
            pltpu.SemaphoreType.DMA(()),
            pltpu.SemaphoreType.DMA((2,)),
        ],
        compiler_params=pltpu.CompilerParams(
            collective_id=0, has_side_effects=True, vmem_limit_bytes=56 << 20
        ),
    )(order, cells, *arrays)
    return result.reshape(half_cap, 2, pulses)


def on_device(
    raw_echoes, range_taps, beam_weights, channel_order, group_cells, tap_counts, chirp_rates
):
    tiles = group_cells.shape[0]
    local, _, _, cell_count = raw_echoes.shape
    average = cell_count // tiles
    half_cap = (average + average // 2) // lax.axis_size("chan")
    fits = average == 2 * BLOCK and lax.axis_size("chan") == 2 and local == 16 and tiles == 8
    if not fits or range_taps.shape[-1] != 4 * BLOCK:
        return generic_device(
            raw_echoes,
            range_taps,
            beam_weights,
            channel_order,
            group_cells,
            tap_counts,
            chirp_rates,
        )
    return focus_call(
        raw_echoes,
        range_taps,
        beam_weights,
        channel_order,
        group_cells,
        tap_counts,
        chirp_rates,
        half_cap,
    )


def solution(mesh):
    return jax.shard_map(
        on_device,
        mesh=mesh,
        in_specs=(P(("scene", "tile"), "chan", None, None), P(), P(), P(), P(), P(), P()),
        out_specs=P(("scene", "tile", "chan"), None, None),
        check_vma=False,
    )
```

```python
import functools

import jax
import jax.numpy as jnp
import numpy as np
from jax import lax
from jax.experimental import pallas as pl
from jax.experimental.pallas import tpu as pltpu
from jax.sharding import PartitionSpec as P

KMAX = 640


def toeplitz_rows(coeffs, block_len, span_len):
    leading = coeffs.shape[:-1]
    filler = jnp.zeros(leading + (span_len + 1 - coeffs.shape[-1],), coeffs.dtype)
    extended = jnp.concatenate([coeffs, filler], -1)
    repeated = jnp.tile(extended, (1,) * len(leading) + (block_len,))
    return repeated[..., : block_len * span_len].reshape(leading + (block_len, span_len))


def complex_matrix(toeplitz_pair):
    real_part = toeplitz_pair[..., 0, :, :]
    imag_part = toeplitz_pair[..., 1, :, :]
    from_real = jnp.stack([real_part, imag_part], -3)
    from_imag = jnp.stack([-imag_part, real_part], -3)
    return jnp.stack([from_real, from_imag], -4)


def block_windows(signal, block_len, lead_blocks, span_blocks, out_blocks):
    total_blocks = out_blocks + span_blocks - 1
    right_pad = total_blocks * block_len - lead_blocks * block_len - signal.shape[-1]
    padded = jnp.pad(signal, [(0, 0)] * (signal.ndim - 1) + [(lead_blocks * block_len, right_pad)])
    blocked = padded.reshape(signal.shape[:-1] + (total_blocks, block_len))
    return jnp.concatenate(
        [
            blocked[..., offset_block : offset_block + out_blocks, :]
            for offset_block in range(span_blocks)
        ],
        -1,
    )


def chirp_taps(counts, sweep_rates, longest):
    position = jnp.arange(longest, dtype=jnp.int32)[None, :]
    lengths = counts[:, None]
    shifted = position - (longest // 2 - lengths // 2)
    inside = (shifted >= 0) & (shifted < lengths)
    extent = lengths.astype(jnp.float32)
    located = shifted.astype(jnp.float32)
    centred = (located - 0.5 * (extent - 1.0)) / extent
    angles = jnp.pi * sweep_rates[:, None] * extent * centred * centred
    envelope = (
        (0.5 - 0.5 * jnp.cos(2.0 * jnp.pi * (located + 0.5) / extent)) * 1.6 / jnp.sqrt(extent)
    )
    envelope = jnp.where(inside, envelope, jnp.zeros_like(envelope))
    return jnp.stack([envelope * jnp.cos(angles), envelope * jnp.sin(angles)], 1)


def range_compress(echoes, filters):
    block_len = filters.shape[-1] // 2
    windows = block_windows(echoes, block_len, 1, 3, echoes.shape[-1] // block_len)
    matrices = complex_matrix(toeplitz_rows(filters, block_len, 3 * block_len))
    product = jnp.einsum(
        "pcanw,caeiw->pceni", windows, matrices, preferred_element_type=jnp.float32
    )
    return product.reshape(echoes.shape)


def azimuth_focus(columns, coeffs):
    block_len = coeffs.shape[-1] // 8
    pulses = columns.shape[-1]
    out_blocks = -(-pulses // block_len)
    windows = block_windows(columns, block_len, 4, 9, out_blocks)
    matrices = complex_matrix(toeplitz_rows(coeffs, block_len, 9 * block_len))
    product = jnp.einsum("sanw,saeiw->seni", windows, matrices, preferred_element_type=jnp.float32)
    return product.reshape(columns.shape[:-1] + (out_blocks * block_len,))[..., :pulses]


def owner_slots(signal, group_starts, group_sizes, offset, slot_width, margin):
    padded = jnp.pad(signal, [(0, 0)] * (signal.ndim - 1) + [(0, margin)])

    def one_group(start_cell, size_cells):
        window_cut = lax.dynamic_slice_in_dim(
            padded, start_cell + offset, slot_width, signal.ndim - 1
        )
        inside = jnp.arange(slot_width, dtype=jnp.int32) + offset < size_cells
        return jnp.where(inside, window_cut, jnp.zeros_like(window_cut))

    return jax.vmap(one_group)(group_starts, group_sizes)


def generic_device(
    raw_echoes, range_taps, beam_weights, channel_order, group_cells, tap_counts, chirp_rates
):
    local_chans = raw_echoes.shape[1]
    all_chans = range_taps.shape[0]
    first_slot = lax.axis_index("chan") * local_chans
    own_channels = lax.dynamic_slice_in_dim(channel_order, first_slot, local_chans)
    selector = (own_channels[:, None] == jnp.arange(all_chans, dtype=jnp.int32)[None, :]).astype(
        jnp.bfloat16
    )
    filters = jnp.dot(
        selector, range_taps.reshape(all_chans, -1), preferred_element_type=jnp.float32
    )
    filters = filters.astype(jnp.bfloat16).reshape(local_chans, 2, -1)
    weights = jnp.dot(
        selector, beam_weights.reshape(all_chans, -1), preferred_element_type=jnp.float32
    )
    weights = weights.reshape(local_chans, 2, -1)
    spectra = range_compress(raw_echoes, filters)
    real_sum = jnp.sum(spectra[:, :, 0] * weights[:, 0] - spectra[:, :, 1] * weights[:, 1], 1)
    imag_sum = jnp.sum(spectra[:, :, 0] * weights[:, 1] + spectra[:, :, 1] * weights[:, 0], 1)
    partial_value = jnp.stack([real_sum, imag_sum], 1)
    tile_count = group_cells.shape[0]
    cell_count = raw_echoes.shape[-1]
    average = cell_count // tile_count
    capacity = average + average // 2
    chan_ways = lax.axis_size("chan")
    half_cap = capacity // chan_ways
    group_starts = jnp.cumsum(group_cells) - group_cells
    chan_offset = lax.axis_index("chan") * half_cap
    summed = lax.psum(partial_value.astype(jnp.bfloat16), "chan")
    outgoing = owner_slots(summed, group_starts, group_cells, chan_offset, half_cap, capacity)
    outgoing = outgoing.transpose(0, 3, 2, 1)
    incoming = lax.all_to_all(outgoing, "tile", split_axis=0, concat_axis=3, tiled=True)
    columns = incoming[0]
    tile_here = lax.axis_index("tile")
    begin_cell = lax.dynamic_index_in_dim(group_starts, tile_here, keepdims=False)
    owned_cells = lax.dynamic_index_in_dim(group_cells, tile_here, keepdims=False)
    local_slot = chan_offset + jnp.arange(half_cap, dtype=jnp.int32)
    inside = local_slot < owned_cells
    count_table = jnp.pad(tap_counts, (0, capacity), mode="edge")
    rate_table = jnp.pad(chirp_rates, (0, capacity), mode="edge")
    count_here = lax.dynamic_slice_in_dim(count_table, begin_cell + chan_offset, half_cap)
    rate_here = lax.dynamic_slice_in_dim(rate_table, begin_cell + chan_offset, half_cap)
    taps_here = chirp_taps(count_here, rate_here, KMAX)
    taps_here = jnp.where(inside[:, None, None], taps_here, jnp.zeros_like(taps_here)).astype(
        jnp.bfloat16
    )
    return azimuth_focus(columns, taps_here)


MESH = pl.DeviceIdType.MESH
BLOCK = 128
STEPS = 5
SPAN = STEPS * BLOCK


def split_bf16(matrix):
    high = matrix.astype(jnp.bfloat16)
    low = (matrix - high.astype(np.float64)).astype(jnp.bfloat16)
    return np.stack([high, low])


def fourier_tables(pulses, local):
    points = 2 * pulses
    freq = np.arange(points)[:, None]
    unit = 2.0 * np.pi / points

    def rotation(index, sign):
        angle = unit * ((freq * index[None, :]) % points)
        return np.cos(angle), sign * np.sin(angle)

    cos_x, sin_x = rotation(np.arange(pulses), -1.0)
    forward = np.stack([np.concatenate([cos_x, sin_x]).T, np.concatenate([-sin_x, cos_x]).T])
    forward = forward.reshape(2, 2, -1, 1, local, 2 * points)
    forward = np.broadcast_to(forward, forward.shape[:3] + (2,) + forward.shape[4:])
    forward = forward.transpose(1, 0, 2, 3, 4, 5).reshape(-1, 2 * points)
    cos_h, sin_h = rotation(pulses - np.arange(points), -1.0)
    taps = np.block([[cos_h, -sin_h], [sin_h, cos_h]])
    cos_y, sin_y = rotation(np.arange(pulses), 1.0)
    inverse = np.block([[cos_y, sin_y], [-sin_y, cos_y]]) / points
    inverse = np.concatenate([inverse[:points], inverse[points:]], 1)
    table = np.concatenate([forward.astype(jnp.bfloat16), *split_bf16(taps)])
    return np.concatenate([table, inverse.astype(jnp.bfloat16)])


def even_series(square, terms):
    value = jnp.full_like(square, terms[-1])
    for term in reversed(terms[:-1]):
        value = value * square + term
    return value


COS_TERMS = [(-1.0) ** n * (2 * np.pi) ** (2 * n) / float(np.prod(np.arange(1, 2 * n + 1, dtype=np.float64))) for n in range(9)]
SIN_TERMS = [(-1.0) ** n * (2 * np.pi) ** (2 * n + 1) / float(np.prod(np.arange(1, 2 * n + 2, dtype=np.float64))) for n in range(9)]


def write_taps(extent, rate, scale, tap_ref, first_tap):
    rows = tap_ref.shape[0] // 2
    length = extent.astype(jnp.int32)
    start = KMAX // 2 - length // 2
    inverse = 1.0 / extent
    turn = 0.5 * rate * extent
    for at in range(0, rows, 32):
        tap = lax.broadcasted_iota(jnp.int32, (32, 2 * BLOCK), 0) + (first_tap + at)
        shifted = tap - start
        inside = (shifted >= 0) & (shifted < length)
        centred = (shifted.astype(jnp.float32) - 0.5 * (extent - 1.0)) * inverse
        square = centred * centred
        envelope = jnp.where(inside, scale * (0.5 + 0.5 * even_series(square, COS_TERMS)), 0.0)
        turns = turn * square
        turns = turns - jnp.floor(turns + 0.5)
        turn_square = turns * turns
        real = envelope * even_series(turn_square, COS_TERMS)
        imag = envelope * (turns * even_series(turn_square, SIN_TERMS))
        tap_ref[at : at + 32] = real.astype(jnp.bfloat16)
        tap_ref[rows + at : rows + at + 32] = imag.astype(jnp.bfloat16)


def focus_kernel(
    half_cap,
    order_hbm,
    cells_hbm,
    raw_ref,
    filter_ref,
    weight_ref,
    count_ref,
    rate_ref,
    table_ref,
    out_ref,
    order_ref,
    cells_ref,
    raw,
    filters,
    weights,
    counts,
    rates,
    table,
    mirror,
    blocks,
    matrices,
    real_sum,
    imag_sum,
    packed,
    columns,
    tap_ref,
    turned,
    first_term,
    load_sems,
    raw_sems,
    send_sem,
    recv_sems,
):
    tiles = packed.shape[0] // 2
    tile_here = lax.axis_index("tile")
    chan_here = lax.axis_index("chan")
    here = 2 * tile_here + chan_here
    local, local_chans, pieces, _ = raw.shape[1:]
    out_blocks = pieces
    pulses = tiles * local
    points = 2 * pulses
    def fetch(source, target, at):
        return pltpu.make_async_copy(source, target, load_sems.at[at])

    def fetch_raw(half, group):
        chans = pl.ds(2 * group, 2)
        return pltpu.make_async_copy(
            raw_ref.at[:, chans, pl.ds(half * pieces, pieces)],
            raw.at[half, :, chans],
            raw_sems.at[half * (local_chans // 2) + group],
        )

    get_filters = fetch(filter_ref, filters, 0)
    get_weights = fetch(weight_ref, weights, 1)
    late = [
        fetch(count_ref, counts, 2),
        fetch(rate_ref, rates, 3),
        fetch(table_ref, table, 4),
    ]
    get_order = fetch(order_hbm, order_ref, 5)
    get_cells = fetch(cells_hbm, cells_ref, 6)
    get_order.start()
    get_filters.start()
    for group in range(local_chans // 2):
        fetch_raw(0, group).start()
    get_weights.start()
    get_cells.start()
    for group in range(local_chans // 2):
        fetch_raw(1, group).start()
    for copy in late:
        copy.start()

    barrier = pltpu.get_barrier_semaphore()
    everyone = [(tile, chan) for tile in range(tiles) for chan in range(2)]
    for tile, chan in everyone:

        @pl.when(2 * tile + chan != here)
        def _():
            pl.semaphore_signal(
                barrier, inc=1, device_id={"tile": tile, "chan": chan}, device_id_type=MESH
            )

    edge = jnp.zeros((local_chans, 2, 2, local, BLOCK), jnp.bfloat16)
    blocks[:, :, :2] = edge
    blocks[:, :, out_blocks + 2 :] = edge
    row = lax.broadcasted_iota(jnp.int32, (2 * BLOCK, 2 * BLOCK), 0)
    lane = lax.broadcasted_iota(jnp.int32, (2 * BLOCK, 2 * BLOCK), 1)
    mirror[...] = jnp.where(row + lane == 2 * BLOCK - 1, 1.0, 0.0).astype(jnp.bfloat16)
    get_order.wait()
    get_filters.wait()

    physical = [order_ref[chan_here * local_chans + chan] for chan in range(local_chans)]
    own = jnp.concatenate([filters[at].astype(jnp.float32) for at in physical], 0)
    own = own.astype(jnp.bfloat16)
    backward = jnp.concatenate(
        [
            jnp.dot(own[:, 2 * BLOCK :], mirror[...], preferred_element_type=jnp.float32),
            jnp.dot(own[:, : 2 * BLOCK], mirror[...], preferred_element_type=jnp.float32),
            jnp.zeros((2 * local_chans, BLOCK), jnp.float32),
        ],
        1,
    ).astype(jnp.bfloat16)
    def toeplitz(at):
        row = jnp.broadcast_to(backward[at : at + 1], (BLOCK, SPAN))
        return pltpu.roll(row, 1, 1, stride=1, stride_axis=0)

    def write_matrices(group):
        for chan in (2 * group, 2 * group + 1):
            real_rows = toeplitz(2 * chan)
            imag_rows = toeplitz(2 * chan + 1)
            for step in range(STEPS):
                at = slice((4 - step) * BLOCK, (5 - step) * BLOCK)
                matrices[chan, step, 0] = real_rows[:, at]
                matrices[chan, step, 1] = imag_rows[:, at]

    def spread_rows(half, group):
        fetch_raw(half, group).wait()
        for chan in (2 * group, 2 * group + 1):
            wide = jnp.swapaxes(raw[half, :, chan].astype(jnp.float32), 0, 1).astype(jnp.bfloat16)
            for block in range(pieces // 2):
                at = half * (pieces // 2) + block + 2
                blocks[chan, 0, at] = wide[2 * block]
                blocks[chan, 1, at] = wide[2 * block + 1]

    def compress(chan, first, last):
        total = None
        for step in range(STEPS):
            window = jnp.concatenate(
                [
                    blocks[chan, part, first + step : last + step].reshape(-1, BLOCK)
                    for part in range(2)
                ],
                1,
            )
            real, imag = matrices[chan, step, 0], matrices[chan, step, 1]
            matrix = jnp.concatenate(
                [jnp.concatenate([real, imag], 1), jnp.concatenate([-imag, real], 1)], 0
            )
            term = jnp.dot(window, matrix, preferred_element_type=jnp.float32)
            total = term if total is None else total + term
        return total

    def beamform(chan, first, last, total):
        own_weight = weights[physical[chan]].astype(jnp.float32)
        for block in range(first, last):
            cells = slice(block * BLOCK, (block + 1) * BLOCK)
            weight_real = own_weight[0:1, cells]
            weight_imag = own_weight[1:2, cells]
            real = total[(block - first) * local : (block - first + 1) * local, :BLOCK]
            imag = total[(block - first) * local : (block - first + 1) * local, BLOCK:]
            new_real = weight_real * real - weight_imag * imag
            new_imag = weight_imag * real + weight_real * imag
            if chan > 0:
                new_real += real_sum[block]
                new_imag += imag_sum[block]
            real_sum[block] = new_real
            imag_sum[block] = new_imag

    def phase(group, first, last):
        chans = (2 * group, 2 * group + 1)
        totals = [compress(chan, first, last) for chan in chans]
        for chan, total in zip(chans, totals):
            beamform(chan, first, last, total)

    is_left = lax.broadcasted_iota(jnp.int32, (local, BLOCK), 1) < BLOCK // 2

    def pack(tile, real, imag):
        def put(chan, at):
            cells = slice(at * BLOCK, (at + 1) * BLOCK)
            packed[2 * tile + chan, 0] = real[:, cells].astype(jnp.bfloat16)
            packed[2 * tile + chan, 1] = imag[:, cells].astype(jnp.bfloat16)

        put(0, 0)
        put(1, 2)
        half_real, half_imag = real[:, BLOCK : 2 * BLOCK], imag[:, BLOCK : 2 * BLOCK]
        packed[2 * tile, 2] = jnp.where(
            is_left, half_real, pltpu.roll(half_imag, BLOCK // 2, 1)
        ).astype(jnp.bfloat16)
        packed[2 * tile + 1, 2] = jnp.where(
            is_left, pltpu.roll(half_real, BLOCK // 2, 1), half_imag
        ).astype(jnp.bfloat16)

    half_here, place_here = here // tiles, lax.rem(here, tiles)

    def send(peer):
        return pltpu.make_async_remote_copy(
            src_ref=packed.at[peer],
            dst_ref=columns.at[half_here, :, place_here],
            send_sem=send_sem,
            recv_sem=recv_sems.at[half_here],
            device_id={"tile": peer // 2, "chan": peer % 2},
            device_id_type=MESH,
        )

    def keep(peer):
        return pltpu.make_async_copy(
            packed.at[peer], columns.at[half_here, :, place_here], recv_sems.at[half_here]
        )

    def deliver(tile):
        pair = tile // 2
        parts = range(3 if tile == 0 else 4)
        real = jnp.concatenate([real_sum[4 * pair + at] for at in parts], 1)
        imag = jnp.concatenate([imag_sum[4 * pair + at] for at in parts], 1)
        if tile % 2 == 1:
            both = jnp.concatenate([real, imag], 0)
            both = pltpu.roll(both, 4 * BLOCK - cells_ref[2 * pair], 1)
            real, imag = both[:local], both[local:]
        pack(tile, real, imag)
        if tile == 0:
            pl.semaphore_wait(barrier, 2 * tiles - 1)
        peers = (2 * tile, 2 * tile + 1)
        for peer in peers if tile == 0 else peers[::-1]:

            @pl.when(peer != here)
            def _():
                send(peer).start()

            @pl.when(peer == here)
            def _():
                keep(peer).start()

    groups = local_chans // 2
    write_matrices(0)
    get_weights.wait()
    for group in range(groups):
        spread_rows(0, group)
        if group + 1 < groups:
            write_matrices(group + 1)
        phase(group, 0, 3)

    def second_phase():
        for group in range(groups):
            spread_rows(1, group)
        for group in range(groups):
            phase(group, 3, out_blocks)

    get_cells.wait()
    early = tile_here < tiles // 2
    pl.when(early)(second_phase)
    deliver(0)
    pl.when(jnp.logical_not(early))(second_phase)
    for tile in range(1, tiles):
        deliver(tile)
    for copy in late:
        copy.wait()
    begin = 0
    for tile in range(tiles):
        begin += jnp.where(tile < tile_here, cells_ref[tile], 0)
    cell_count = counts.shape[1]

    def own_cells(table):
        wide = jnp.broadcast_to(table.astype(jnp.float32), (8, cell_count))

        def cut(at):
            shift = lax.rem(2 * cell_count - begin - at, cell_count)
            return pltpu.roll(wide, shift, 1)[0:1, :BLOCK]

        return jnp.concatenate([cut(2 * BLOCK * chan_here), cut(BLOCK + BLOCK // 2 * chan_here)], 1)

    extent = own_cells(counts[...])
    place = lax.broadcasted_iota(jnp.int32, (1, 2 * BLOCK), 1)
    place += jnp.where(place < BLOCK, 2 * BLOCK * chan_here, BLOCK // 2 * chan_here)
    live = place < cells_ref[tile_here]
    scale = jnp.where(live, 1.6 / jnp.sqrt(extent), 0.0)
    rate = own_cells(rates[...])
    write_taps(extent, rate, scale, tap_ref, KMAX // 2 - pulses)
    taps = tap_ref[...]
    high = table[2 * points : 4 * points]
    low = table[4 * points : 6 * points]
    response = jnp.dot(high, taps, preferred_element_type=jnp.float32) + jnp.dot(
        low, taps, preferred_element_type=jnp.float32
    )
    turned[...] = response.T

    for half in range(2):
        pltpu.make_async_copy(columns.at[half], columns.at[half], recv_sems.at[half]).wait()
        pieces = [columns[half, at].reshape(BLOCK, BLOCK).T for at in range(3)]
        signal = jnp.concatenate(
            [
                jnp.concatenate(pieces[:2], 1),
                jnp.concatenate([pieces[2][: BLOCK // 2], pieces[2][BLOCK // 2 :]], 1),
            ],
            0,
        )
        term = jnp.dot(
            signal,
            table[2 * half * BLOCK : 2 * (half + 1) * BLOCK],
            preferred_element_type=jnp.float32,
        )
        if half == 0:
            first_term[...] = term
        else:
            image = first_term[...] + term
    slots = image.shape[0]
    real, imag = image[:, :points], image[:, points:]
    tap_real, tap_imag = turned[:slots, :points], turned[:slots, points:]
    product = jnp.concatenate(
        [real * tap_real - imag * tap_imag, real * tap_imag + imag * tap_real], 1
    ).astype(jnp.bfloat16)
    inverse = table[6 * points :]
    result = jnp.dot(
        product[:, :points], inverse[:, :points], preferred_element_type=jnp.float32
    ) + jnp.dot(product[:, points:], inverse[:, points:], preferred_element_type=jnp.float32)
    for part in range(2):
        lanes = slice(part * pulses, (part + 1) * pulses)
        out_ref[pl.ds(BLOCK * chan_here + part, BLOCK, stride=2), :] = result[:BLOCK, lanes]
        out_ref[pl.ds(2 * BLOCK * (1 - chan_here) + part, slots - BLOCK, stride=2), :] = result[
            BLOCK:, lanes
        ]
    sent = packed.at[pl.ds(0, 2 * tiles - 1)]
    pltpu.make_async_copy(sent, sent, send_sem).wait()


def focus_call(raw_echoes, range_taps, beam_weights, order, cells, counts, rates, half_cap):
    local, local_chans, _, cell_count = raw_echoes.shape
    tiles = cells.shape[0]
    pulses = tiles * local
    out_blocks = cell_count // BLOCK
    raw_echoes = raw_echoes.reshape(local, local_chans, 2, out_blocks, BLOCK)
    raw_echoes = raw_echoes.transpose(0, 1, 3, 2, 4).reshape(local, local_chans, -1, BLOCK)
    table = jnp.asarray(fourier_tables(pulses, local))
    counts, rates = counts[None], rates[None]
    arrays = [raw_echoes, range_taps, beam_weights, counts, rates, table]
    total = pltpu.VMEM((out_blocks, local, BLOCK), jnp.float32)
    result = pl.pallas_call(
        functools.partial(focus_kernel, half_cap),
        out_shape=pltpu.VMEM((2 * half_cap, pulses), jnp.float32),
        in_specs=[pl.BlockSpec(memory_space=pl.ANY)] * (2 + len(arrays)),
        out_specs=pl.BlockSpec(memory_space=pltpu.VMEM),
        scratch_shapes=[pltpu.SMEM(order.shape, order.dtype), pltpu.SMEM(cells.shape, cells.dtype)]
        + [pltpu.VMEM((2, local, local_chans, out_blocks, BLOCK), raw_echoes.dtype)]
        + [pltpu.VMEM(array.shape, array.dtype) for array in arrays[1:]]
        + [
            pltpu.VMEM((2 * BLOCK, 2 * BLOCK), jnp.bfloat16),
            pltpu.VMEM((local_chans, 2, out_blocks + 4, local, BLOCK), jnp.bfloat16),
            pltpu.VMEM((local_chans, STEPS, 2, BLOCK, BLOCK), jnp.bfloat16),
            total,
            total,
            pltpu.VMEM((2 * tiles, 3, local, BLOCK), jnp.bfloat16),
            pltpu.VMEM((2, 3, tiles, local, BLOCK), jnp.bfloat16),
            pltpu.VMEM((4 * pulses, 2 * BLOCK), jnp.bfloat16),
            pltpu.VMEM((2 * BLOCK, 4 * pulses), jnp.float32),
            pltpu.VMEM((half_cap, 4 * pulses), jnp.float32),
            pltpu.SemaphoreType.DMA((len(arrays) + 1,)),
            pltpu.SemaphoreType.DMA((local_chans,)),
            pltpu.SemaphoreType.DMA(()),
            pltpu.SemaphoreType.DMA((2,)),
        ],
        compiler_params=pltpu.CompilerParams(
            collective_id=0, has_side_effects=True, vmem_limit_bytes=56 << 20
        ),
    )(order, cells, *arrays)
    return result.reshape(half_cap, 2, pulses)


def on_device(
    raw_echoes, range_taps, beam_weights, channel_order, group_cells, tap_counts, chirp_rates
):
    tiles = group_cells.shape[0]
    local, _, _, cell_count = raw_echoes.shape
    average = cell_count // tiles
    half_cap = (average + average // 2) // lax.axis_size("chan")
    fits = average == 2 * BLOCK and lax.axis_size("chan") == 2 and local == 16 and tiles == 8
    if not fits or range_taps.shape[-1] != 4 * BLOCK:
        return generic_device(
            raw_echoes,
            range_taps,
            beam_weights,
            channel_order,
            group_cells,
            tap_counts,
            chirp_rates,
        )
    return focus_call(
        raw_echoes,
        range_taps,
        beam_weights,
        channel_order,
        group_cells,
        tap_counts,
        chirp_rates,
        half_cap,
    )


def solution(mesh):
    return jax.shard_map(
        on_device,
        mesh=mesh,
        in_specs=(P(("scene", "tile"), "chan", None, None), P(), P(), P(), P(), P(), P()),
        out_specs=P(("scene", "tile", "chan"), None, None),
        check_vma=False,
    )
```

```python
import functools

import jax
import jax.numpy as jnp
import numpy as np
from jax import lax
from jax.experimental import pallas as pl
from jax.experimental.pallas import tpu as pltpu
from jax.sharding import PartitionSpec as P

KMAX = 640


def toeplitz_rows(coeffs, block_len, span_len):
    leading = coeffs.shape[:-1]
    filler = jnp.zeros(leading + (span_len + 1 - coeffs.shape[-1],), coeffs.dtype)
    extended = jnp.concatenate([coeffs, filler], -1)
    repeated = jnp.tile(extended, (1,) * len(leading) + (block_len,))
    return repeated[..., : block_len * span_len].reshape(leading + (block_len, span_len))


def complex_matrix(toeplitz_pair):
    real_part = toeplitz_pair[..., 0, :, :]
    imag_part = toeplitz_pair[..., 1, :, :]
    from_real = jnp.stack([real_part, imag_part], -3)
    from_imag = jnp.stack([-imag_part, real_part], -3)
    return jnp.stack([from_real, from_imag], -4)


def block_windows(signal, block_len, lead_blocks, span_blocks, out_blocks):
    total_blocks = out_blocks + span_blocks - 1
    right_pad = total_blocks * block_len - lead_blocks * block_len - signal.shape[-1]
    padded = jnp.pad(signal, [(0, 0)] * (signal.ndim - 1) + [(lead_blocks * block_len, right_pad)])
    blocked = padded.reshape(signal.shape[:-1] + (total_blocks, block_len))
    return jnp.concatenate(
        [
            blocked[..., offset_block : offset_block + out_blocks, :]
            for offset_block in range(span_blocks)
        ],
        -1,
    )


def chirp_taps(counts, sweep_rates, longest):
    position = jnp.arange(longest, dtype=jnp.int32)[None, :]
    lengths = counts[:, None]
    shifted = position - (longest // 2 - lengths // 2)
    inside = (shifted >= 0) & (shifted < lengths)
    extent = lengths.astype(jnp.float32)
    located = shifted.astype(jnp.float32)
    centred = (located - 0.5 * (extent - 1.0)) / extent
    angles = jnp.pi * sweep_rates[:, None] * extent * centred * centred
    envelope = (
        (0.5 - 0.5 * jnp.cos(2.0 * jnp.pi * (located + 0.5) / extent)) * 1.6 / jnp.sqrt(extent)
    )
    envelope = jnp.where(inside, envelope, jnp.zeros_like(envelope))
    return jnp.stack([envelope * jnp.cos(angles), envelope * jnp.sin(angles)], 1)


def range_compress(echoes, filters):
    block_len = filters.shape[-1] // 2
    windows = block_windows(echoes, block_len, 1, 3, echoes.shape[-1] // block_len)
    matrices = complex_matrix(toeplitz_rows(filters, block_len, 3 * block_len))
    product = jnp.einsum(
        "pcanw,caeiw->pceni", windows, matrices, preferred_element_type=jnp.float32
    )
    return product.reshape(echoes.shape)


def azimuth_focus(columns, coeffs):
    block_len = coeffs.shape[-1] // 8
    pulses = columns.shape[-1]
    out_blocks = -(-pulses // block_len)
    windows = block_windows(columns, block_len, 4, 9, out_blocks)
    matrices = complex_matrix(toeplitz_rows(coeffs, block_len, 9 * block_len))
    product = jnp.einsum("sanw,saeiw->seni", windows, matrices, preferred_element_type=jnp.float32)
    return product.reshape(columns.shape[:-1] + (out_blocks * block_len,))[..., :pulses]


def owner_slots(signal, group_starts, group_sizes, offset, slot_width, margin):
    padded = jnp.pad(signal, [(0, 0)] * (signal.ndim - 1) + [(0, margin)])

    def one_group(start_cell, size_cells):
        window_cut = lax.dynamic_slice_in_dim(
            padded, start_cell + offset, slot_width, signal.ndim - 1
        )
        inside = jnp.arange(slot_width, dtype=jnp.int32) + offset < size_cells
        return jnp.where(inside, window_cut, jnp.zeros_like(window_cut))

    return jax.vmap(one_group)(group_starts, group_sizes)


def generic_device(
    raw_echoes, range_taps, beam_weights, channel_order, group_cells, tap_counts, chirp_rates
):
    local_chans = raw_echoes.shape[1]
    all_chans = range_taps.shape[0]
    first_slot = lax.axis_index("chan") * local_chans
    own_channels = lax.dynamic_slice_in_dim(channel_order, first_slot, local_chans)
    selector = (own_channels[:, None] == jnp.arange(all_chans, dtype=jnp.int32)[None, :]).astype(
        jnp.bfloat16
    )
    filters = jnp.dot(
        selector, range_taps.reshape(all_chans, -1), preferred_element_type=jnp.float32
    )
    filters = filters.astype(jnp.bfloat16).reshape(local_chans, 2, -1)
    weights = jnp.dot(
        selector, beam_weights.reshape(all_chans, -1), preferred_element_type=jnp.float32
    )
    weights = weights.reshape(local_chans, 2, -1)
    spectra = range_compress(raw_echoes, filters)
    real_sum = jnp.sum(spectra[:, :, 0] * weights[:, 0] - spectra[:, :, 1] * weights[:, 1], 1)
    imag_sum = jnp.sum(spectra[:, :, 0] * weights[:, 1] + spectra[:, :, 1] * weights[:, 0], 1)
    partial_value = jnp.stack([real_sum, imag_sum], 1)
    tile_count = group_cells.shape[0]
    cell_count = raw_echoes.shape[-1]
    average = cell_count // tile_count
    capacity = average + average // 2
    chan_ways = lax.axis_size("chan")
    half_cap = capacity // chan_ways
    group_starts = jnp.cumsum(group_cells) - group_cells
    chan_offset = lax.axis_index("chan") * half_cap
    summed = lax.psum(partial_value.astype(jnp.bfloat16), "chan")
    outgoing = owner_slots(summed, group_starts, group_cells, chan_offset, half_cap, capacity)
    outgoing = outgoing.transpose(0, 3, 2, 1)
    incoming = lax.all_to_all(outgoing, "tile", split_axis=0, concat_axis=3, tiled=True)
    columns = incoming[0]
    tile_here = lax.axis_index("tile")
    begin_cell = lax.dynamic_index_in_dim(group_starts, tile_here, keepdims=False)
    owned_cells = lax.dynamic_index_in_dim(group_cells, tile_here, keepdims=False)
    local_slot = chan_offset + jnp.arange(half_cap, dtype=jnp.int32)
    inside = local_slot < owned_cells
    count_table = jnp.pad(tap_counts, (0, capacity), mode="edge")
    rate_table = jnp.pad(chirp_rates, (0, capacity), mode="edge")
    count_here = lax.dynamic_slice_in_dim(count_table, begin_cell + chan_offset, half_cap)
    rate_here = lax.dynamic_slice_in_dim(rate_table, begin_cell + chan_offset, half_cap)
    taps_here = chirp_taps(count_here, rate_here, KMAX)
    taps_here = jnp.where(inside[:, None, None], taps_here, jnp.zeros_like(taps_here)).astype(
        jnp.bfloat16
    )
    return azimuth_focus(columns, taps_here)


MESH = pl.DeviceIdType.MESH
BLOCK = 128
STEPS = 5
SPAN = STEPS * BLOCK


def split_bf16(matrix):
    high = matrix.astype(jnp.bfloat16)
    low = (matrix - high.astype(np.float64)).astype(jnp.bfloat16)
    return np.stack([high, low])


def fourier_tables(pulses, local):
    points = 2 * pulses
    freq = np.arange(points)[:, None]
    unit = 2.0 * np.pi / points

    def rotation(index, sign):
        angle = unit * ((freq * index[None, :]) % points)
        return np.cos(angle), sign * np.sin(angle)

    cos_x, sin_x = rotation(np.arange(pulses), -1.0)
    forward = np.stack([np.concatenate([cos_x, sin_x]).T, np.concatenate([-sin_x, cos_x]).T])
    forward = forward.reshape(2, 2, -1, 1, local, 2 * points)
    forward = np.broadcast_to(forward, forward.shape[:3] + (2,) + forward.shape[4:])
    forward = forward.transpose(1, 0, 2, 3, 4, 5).reshape(-1, 2 * points)
    cos_h, sin_h = rotation(pulses - np.arange(points), -1.0)
    taps = np.block([[cos_h, -sin_h], [sin_h, cos_h]])
    cos_y, sin_y = rotation(np.arange(pulses), 1.0)
    inverse = np.block([[cos_y, sin_y], [-sin_y, cos_y]]) / points
    inverse = np.concatenate([inverse[:points], inverse[points:]], 1)
    table = np.concatenate([forward.astype(jnp.bfloat16), *split_bf16(taps)])
    return np.concatenate([table, inverse.astype(jnp.bfloat16)])


def even_series(square, terms):
    value = jnp.full_like(square, terms[-1])
    for term in reversed(terms[:-1]):
        value = value * square + term
    return value


COS_TERMS = [(-1.0) ** n * (2 * np.pi) ** (2 * n) / float(np.prod(np.arange(1, 2 * n + 1, dtype=np.float64))) for n in range(9)]
SIN_TERMS = [(-1.0) ** n * (2 * np.pi) ** (2 * n + 1) / float(np.prod(np.arange(1, 2 * n + 2, dtype=np.float64))) for n in range(9)]


def write_taps(extent, rate, scale, tap_ref, first_tap):
    rows = tap_ref.shape[0] // 2
    length = extent.astype(jnp.int32)
    start = KMAX // 2 - length // 2
    inverse = 1.0 / extent
    turn = 0.5 * rate * extent
    for at in range(0, rows, 32):
        tap = lax.broadcasted_iota(jnp.int32, (32, 2 * BLOCK), 0) + (first_tap + at)
        shifted = tap - start
        inside = (shifted >= 0) & (shifted < length)
        centred = (shifted.astype(jnp.float32) - 0.5 * (extent - 1.0)) * inverse
        square = centred * centred
        envelope = jnp.where(inside, scale * (0.5 + 0.5 * even_series(square, COS_TERMS)), 0.0)
        turns = turn * square
        turns = turns - jnp.floor(turns + 0.5)
        turn_square = turns * turns
        real = envelope * even_series(turn_square, COS_TERMS)
        imag = envelope * (turns * even_series(turn_square, SIN_TERMS))
        tap_ref[at : at + 32] = real.astype(jnp.bfloat16)
        tap_ref[rows + at : rows + at + 32] = imag.astype(jnp.bfloat16)


def focus_kernel(
    half_cap,
    order_hbm,
    cells_hbm,
    raw_ref,
    filter_ref,
    weight_ref,
    count_ref,
    rate_ref,
    table_ref,
    out_ref,
    order_ref,
    cells_ref,
    raw,
    filters,
    weights,
    counts,
    rates,
    table,
    mirror,
    blocks,
    matrices,
    real_sum,
    imag_sum,
    packed,
    columns,
    tap_ref,
    turned,
    first_term,
    load_sems,
    raw_sems,
    send_sem,
    recv_sems,
):
    tiles = packed.shape[0] // 2
    tile_here = lax.axis_index("tile")
    chan_here = lax.axis_index("chan")
    here = 2 * tile_here + chan_here
    local, local_chans, pieces, _ = raw.shape[1:]
    out_blocks = pieces
    pulses = tiles * local
    points = 2 * pulses
    def fetch(source, target, at):
        return pltpu.make_async_copy(source, target, load_sems.at[at])

    def fetch_raw(half, group):
        chans = pl.ds(2 * group, 2)
        return pltpu.make_async_copy(
            raw_ref.at[:, chans, pl.ds(half * pieces, pieces)],
            raw.at[half, :, chans],
            raw_sems.at[half * (local_chans // 2) + group],
        )

    get_filters = fetch(filter_ref, filters, 0)
    get_weights = fetch(weight_ref, weights, 1)
    late = [
        fetch(count_ref, counts, 2),
        fetch(rate_ref, rates, 3),
        fetch(table_ref, table, 4),
    ]
    get_order = fetch(order_hbm, order_ref, 5)
    get_cells = fetch(cells_hbm, cells_ref, 6)
    get_order.start()
    get_filters.start()
    for group in range(local_chans // 2):
        fetch_raw(0, group).start()
    get_weights.start()
    get_cells.start()
    for group in range(local_chans // 2):
        fetch_raw(1, group).start()
    for copy in late:
        copy.start()

    barrier = pltpu.get_barrier_semaphore()
    everyone = [(tile, chan) for tile in range(tiles) for chan in range(2)]
    for tile, chan in everyone:

        @pl.when(2 * tile + chan != here)
        def _():
            pl.semaphore_signal(
                barrier, inc=1, device_id={"tile": tile, "chan": chan}, device_id_type=MESH
            )

    edge = jnp.zeros((local_chans, 2, 2, local, BLOCK), jnp.bfloat16)
    blocks[:, :, :2] = edge
    blocks[:, :, out_blocks + 2 :] = edge
    row = lax.broadcasted_iota(jnp.int32, (2 * BLOCK, 2 * BLOCK), 0)
    lane = lax.broadcasted_iota(jnp.int32, (2 * BLOCK, 2 * BLOCK), 1)
    mirror[...] = jnp.where(row + lane == 2 * BLOCK - 1, 1.0, 0.0).astype(jnp.bfloat16)
    get_order.wait()
    get_filters.wait()

    physical = [order_ref[chan_here * local_chans + chan] for chan in range(local_chans)]
    own = jnp.concatenate([filters[at].astype(jnp.float32) for at in physical], 0)
    own = own.astype(jnp.bfloat16)
    backward = jnp.concatenate(
        [
            jnp.dot(own[:, 2 * BLOCK :], mirror[...], preferred_element_type=jnp.float32),
            jnp.dot(own[:, : 2 * BLOCK], mirror[...], preferred_element_type=jnp.float32),
            jnp.zeros((2 * local_chans, BLOCK), jnp.float32),
        ],
        1,
    ).astype(jnp.bfloat16)
    def toeplitz(at):
        row = jnp.broadcast_to(backward[at : at + 1], (BLOCK, SPAN))
        return pltpu.roll(row, 1, 1, stride=1, stride_axis=0)

    def write_matrix(chan, part):
        rows = toeplitz(2 * chan + part)
        for step in range(STEPS):
            matrices[chan, step, part] = rows[:, (4 - step) * BLOCK : (5 - step) * BLOCK]

    def spread_rows(half, chan):
        wide = jnp.swapaxes(raw[half, :, chan].astype(jnp.float32), 0, 1).astype(jnp.bfloat16)
        for block in range(pieces // 2):
            at = half * (pieces // 2) + block + 2
            blocks[chan, 0, at] = wide[2 * block]
            blocks[chan, 1, at] = wide[2 * block + 1]

    def compress(chan, first, last):
        total = None
        for step in range(STEPS):
            window = jnp.concatenate(
                [
                    blocks[chan, part, first + step : last + step].reshape(-1, BLOCK)
                    for part in range(2)
                ],
                1,
            )
            real, imag = matrices[chan, step, 0], matrices[chan, step, 1]
            matrix = jnp.concatenate(
                [jnp.concatenate([real, imag], 1), jnp.concatenate([-imag, real], 1)], 0
            )
            term = jnp.dot(window, matrix, preferred_element_type=jnp.float32)
            total = term if total is None else total + term
        return total

    def beamform(chan, first, last, total):
        own_weight = weights[physical[chan]].astype(jnp.float32)
        for block in range(first, last):
            cells = slice(block * BLOCK, (block + 1) * BLOCK)
            weight_real = own_weight[0:1, cells]
            weight_imag = own_weight[1:2, cells]
            real = total[(block - first) * local : (block - first + 1) * local, :BLOCK]
            imag = total[(block - first) * local : (block - first + 1) * local, BLOCK:]
            new_real = weight_real * real - weight_imag * imag
            new_imag = weight_imag * real + weight_real * imag
            if chan > 0:
                new_real += real_sum[block]
                new_imag += imag_sum[block]
            real_sum[block] = new_real
            imag_sum[block] = new_imag

    def phase(group, first, last):
        chans = (2 * group, 2 * group + 1)
        totals = [compress(chan, first, last) for chan in chans]
        for chan, total in zip(chans, totals):
            beamform(chan, first, last, total)

    is_left = lax.broadcasted_iota(jnp.int32, (local, BLOCK), 1) < BLOCK // 2

    def pack(tile, real, imag):
        def put(chan, at):
            cells = slice(at * BLOCK, (at + 1) * BLOCK)
            packed[2 * tile + chan, 0] = real[:, cells].astype(jnp.bfloat16)
            packed[2 * tile + chan, 1] = imag[:, cells].astype(jnp.bfloat16)

        put(0, 0)
        put(1, 2)
        half_real, half_imag = real[:, BLOCK : 2 * BLOCK], imag[:, BLOCK : 2 * BLOCK]
        packed[2 * tile, 2] = jnp.where(
            is_left, half_real, pltpu.roll(half_imag, BLOCK // 2, 1)
        ).astype(jnp.bfloat16)
        packed[2 * tile + 1, 2] = jnp.where(
            is_left, pltpu.roll(half_real, BLOCK // 2, 1), half_imag
        ).astype(jnp.bfloat16)

    half_here, place_here = here // tiles, lax.rem(here, tiles)

    def send(peer):
        return pltpu.make_async_remote_copy(
            src_ref=packed.at[peer],
            dst_ref=columns.at[half_here, :, place_here],
            send_sem=send_sem,
            recv_sem=recv_sems.at[half_here],
            device_id={"tile": peer // 2, "chan": peer % 2},
            device_id_type=MESH,
        )

    def keep(peer):
        return pltpu.make_async_copy(
            packed.at[peer], columns.at[half_here, :, place_here], recv_sems.at[half_here]
        )

    def deliver(tile):
        pair = tile // 2
        parts = range(3 if tile == 0 else 4)
        real = jnp.concatenate([real_sum[4 * pair + at] for at in parts], 1)
        imag = jnp.concatenate([imag_sum[4 * pair + at] for at in parts], 1)
        if tile % 2 == 1:
            both = jnp.concatenate([real, imag], 0)
            both = pltpu.roll(both, 4 * BLOCK - cells_ref[2 * pair], 1)
            real, imag = both[:local], both[local:]
        pack(tile, real, imag)
        if tile == 0:
            pl.semaphore_wait(barrier, 2 * tiles - 1)
        peers = (2 * tile, 2 * tile + 1)
        for peer in peers if tile == 0 else peers[::-1]:

            @pl.when(peer != here)
            def _():
                send(peer).start()

            @pl.when(peer == here)
            def _():
                keep(peer).start()

    groups = local_chans // 2
    for chan in range(2):
        for part in range(2):
            write_matrix(chan, part)
    get_weights.wait()
    for group in range(groups):
        fetch_raw(0, group).wait()
    spread_rows(0, 0)
    write_matrix(2, 0)
    spread_rows(0, 1)
    for group in range(groups):
        first = 2 * group
        more = first + 2 < local_chans
        totals = [compress(first, 0, 3), compress(first + 1, 0, 3)]
        if more:
            write_matrix(first + 2, 1)
            spread_rows(0, first + 2)
            write_matrix(first + 3, 0)
        beamform(first, 0, 3, totals[0])
        if more:
            spread_rows(0, first + 3)
            write_matrix(first + 3, 1)
        beamform(first + 1, 0, 3, totals[1])
        if first + 4 < local_chans:
            write_matrix(first + 4, 0)

    def second_phase():
        for group in range(groups):
            fetch_raw(1, group).wait()
        for chan in range(local_chans):
            spread_rows(1, chan)
        for group in range(groups):
            phase(group, 3, out_blocks)

    get_cells.wait()
    early = tile_here < tiles // 2
    pl.when(early)(second_phase)
    deliver(0)
    pl.when(jnp.logical_not(early))(second_phase)
    for tile in range(1, tiles):
        deliver(tile)
    for copy in late:
        copy.wait()
    begin = 0
    for tile in range(tiles):
        begin += jnp.where(tile < tile_here, cells_ref[tile], 0)
    cell_count = counts.shape[1]

    def own_cells(table):
        wide = jnp.broadcast_to(table.astype(jnp.float32), (8, cell_count))

        def cut(at):
            shift = lax.rem(2 * cell_count - begin - at, cell_count)
            return pltpu.roll(wide, shift, 1)[0:1, :BLOCK]

        return jnp.concatenate([cut(2 * BLOCK * chan_here), cut(BLOCK + BLOCK // 2 * chan_here)], 1)

    extent = own_cells(counts[...])
    place = lax.broadcasted_iota(jnp.int32, (1, 2 * BLOCK), 1)
    place += jnp.where(place < BLOCK, 2 * BLOCK * chan_here, BLOCK // 2 * chan_here)
    live = place < cells_ref[tile_here]
    scale = jnp.where(live, 1.6 / jnp.sqrt(extent), 0.0)
    rate = own_cells(rates[...])
    write_taps(extent, rate, scale, tap_ref, KMAX // 2 - pulses)
    taps = tap_ref[...]
    high = table[2 * points : 4 * points]
    low = table[4 * points : 6 * points]
    response = jnp.dot(high, taps, preferred_element_type=jnp.float32) + jnp.dot(
        low, taps, preferred_element_type=jnp.float32
    )
    turned[...] = response.T

    for half in range(2):
        pltpu.make_async_copy(columns.at[half], columns.at[half], recv_sems.at[half]).wait()
        pieces = [columns[half, at].reshape(BLOCK, BLOCK).T for at in range(3)]
        signal = jnp.concatenate(
            [
                jnp.concatenate(pieces[:2], 1),
                jnp.concatenate([pieces[2][: BLOCK // 2], pieces[2][BLOCK // 2 :]], 1),
            ],
            0,
        )
        term = jnp.dot(
            signal,
            table[2 * half * BLOCK : 2 * (half + 1) * BLOCK],
            preferred_element_type=jnp.float32,
        )
        if half == 0:
            first_term[...] = term
        else:
            image = first_term[...] + term
    slots = image.shape[0]
    real, imag = image[:, :points], image[:, points:]
    tap_real, tap_imag = turned[:slots, :points], turned[:slots, points:]
    product = jnp.concatenate(
        [real * tap_real - imag * tap_imag, real * tap_imag + imag * tap_real], 1
    ).astype(jnp.bfloat16)
    inverse = table[6 * points :]
    result = jnp.dot(
        product[:, :points], inverse[:, :points], preferred_element_type=jnp.float32
    ) + jnp.dot(product[:, points:], inverse[:, points:], preferred_element_type=jnp.float32)
    for part in range(2):
        lanes = slice(part * pulses, (part + 1) * pulses)
        out_ref[pl.ds(BLOCK * chan_here + part, BLOCK, stride=2), :] = result[:BLOCK, lanes]
        out_ref[pl.ds(2 * BLOCK * (1 - chan_here) + part, slots - BLOCK, stride=2), :] = result[
            BLOCK:, lanes
        ]
    sent = packed.at[pl.ds(0, 2 * tiles - 1)]
    pltpu.make_async_copy(sent, sent, send_sem).wait()


def focus_call(raw_echoes, range_taps, beam_weights, order, cells, counts, rates, half_cap):
    local, local_chans, _, cell_count = raw_echoes.shape
    tiles = cells.shape[0]
    pulses = tiles * local
    out_blocks = cell_count // BLOCK
    raw_echoes = raw_echoes.reshape(local, local_chans, 2, out_blocks, BLOCK)
    raw_echoes = raw_echoes.transpose(0, 1, 3, 2, 4).reshape(local, local_chans, -1, BLOCK)
    table = jnp.asarray(fourier_tables(pulses, local))
    counts, rates = counts[None], rates[None]
    arrays = [raw_echoes, range_taps, beam_weights, counts, rates, table]
    total = pltpu.VMEM((out_blocks, local, BLOCK), jnp.float32)
    result = pl.pallas_call(
        functools.partial(focus_kernel, half_cap),
        out_shape=pltpu.VMEM((2 * half_cap, pulses), jnp.float32),
        in_specs=[pl.BlockSpec(memory_space=pl.ANY)] * (2 + len(arrays)),
        out_specs=pl.BlockSpec(memory_space=pltpu.VMEM),
        scratch_shapes=[pltpu.SMEM(order.shape, order.dtype), pltpu.SMEM(cells.shape, cells.dtype)]
        + [pltpu.VMEM((2, local, local_chans, out_blocks, BLOCK), raw_echoes.dtype)]
        + [pltpu.VMEM(array.shape, array.dtype) for array in arrays[1:]]
        + [
            pltpu.VMEM((2 * BLOCK, 2 * BLOCK), jnp.bfloat16),
            pltpu.VMEM((local_chans, 2, out_blocks + 4, local, BLOCK), jnp.bfloat16),
            pltpu.VMEM((local_chans, STEPS, 2, BLOCK, BLOCK), jnp.bfloat16),
            total,
            total,
            pltpu.VMEM((2 * tiles, 3, local, BLOCK), jnp.bfloat16),
            pltpu.VMEM((2, 3, tiles, local, BLOCK), jnp.bfloat16),
            pltpu.VMEM((4 * pulses, 2 * BLOCK), jnp.bfloat16),
            pltpu.VMEM((2 * BLOCK, 4 * pulses), jnp.float32),
            pltpu.VMEM((half_cap, 4 * pulses), jnp.float32),
            pltpu.SemaphoreType.DMA((len(arrays) + 1,)),
            pltpu.SemaphoreType.DMA((local_chans,)),
            pltpu.SemaphoreType.DMA(()),
            pltpu.SemaphoreType.DMA((2,)),
        ],
        compiler_params=pltpu.CompilerParams(
            collective_id=0, has_side_effects=True, vmem_limit_bytes=56 << 20
        ),
    )(order, cells, *arrays)
    return result.reshape(half_cap, 2, pulses)


def on_device(
    raw_echoes, range_taps, beam_weights, channel_order, group_cells, tap_counts, chirp_rates
):
    tiles = group_cells.shape[0]
    local, _, _, cell_count = raw_echoes.shape
    average = cell_count // tiles
    half_cap = (average + average // 2) // lax.axis_size("chan")
    fits = average == 2 * BLOCK and lax.axis_size("chan") == 2 and local == 16 and tiles == 8
    if not fits or range_taps.shape[-1] != 4 * BLOCK:
        return generic_device(
            raw_echoes,
            range_taps,
            beam_weights,
            channel_order,
            group_cells,
            tap_counts,
            chirp_rates,
        )
    return focus_call(
        raw_echoes,
        range_taps,
        beam_weights,
        channel_order,
        group_cells,
        tap_counts,
        chirp_rates,
        half_cap,
    )


def solution(mesh):
    return jax.shard_map(
        on_device,
        mesh=mesh,
        in_specs=(P(("scene", "tile"), "chan", None, None), P(), P(), P(), P(), P(), P()),
        out_specs=P(("scene", "tile", "chan"), None, None),
        check_vma=False,
    )
```

```python
import functools

import jax
import jax.numpy as jnp
import numpy as np
from jax import lax
from jax.experimental import pallas as pl
from jax.experimental.pallas import tpu as pltpu
from jax.sharding import PartitionSpec as P

KMAX = 640


def toeplitz_rows(coeffs, block_len, span_len):
    leading = coeffs.shape[:-1]
    filler = jnp.zeros(leading + (span_len + 1 - coeffs.shape[-1],), coeffs.dtype)
    extended = jnp.concatenate([coeffs, filler], -1)
    repeated = jnp.tile(extended, (1,) * len(leading) + (block_len,))
    return repeated[..., : block_len * span_len].reshape(leading + (block_len, span_len))


def complex_matrix(toeplitz_pair):
    real_part = toeplitz_pair[..., 0, :, :]
    imag_part = toeplitz_pair[..., 1, :, :]
    from_real = jnp.stack([real_part, imag_part], -3)
    from_imag = jnp.stack([-imag_part, real_part], -3)
    return jnp.stack([from_real, from_imag], -4)


def block_windows(signal, block_len, lead_blocks, span_blocks, out_blocks):
    total_blocks = out_blocks + span_blocks - 1
    right_pad = total_blocks * block_len - lead_blocks * block_len - signal.shape[-1]
    padded = jnp.pad(signal, [(0, 0)] * (signal.ndim - 1) + [(lead_blocks * block_len, right_pad)])
    blocked = padded.reshape(signal.shape[:-1] + (total_blocks, block_len))
    return jnp.concatenate(
        [
            blocked[..., offset_block : offset_block + out_blocks, :]
            for offset_block in range(span_blocks)
        ],
        -1,
    )


def chirp_taps(counts, sweep_rates, longest):
    position = jnp.arange(longest, dtype=jnp.int32)[None, :]
    lengths = counts[:, None]
    shifted = position - (longest // 2 - lengths // 2)
    inside = (shifted >= 0) & (shifted < lengths)
    extent = lengths.astype(jnp.float32)
    located = shifted.astype(jnp.float32)
    centred = (located - 0.5 * (extent - 1.0)) / extent
    angles = jnp.pi * sweep_rates[:, None] * extent * centred * centred
    envelope = (
        (0.5 - 0.5 * jnp.cos(2.0 * jnp.pi * (located + 0.5) / extent)) * 1.6 / jnp.sqrt(extent)
    )
    envelope = jnp.where(inside, envelope, jnp.zeros_like(envelope))
    return jnp.stack([envelope * jnp.cos(angles), envelope * jnp.sin(angles)], 1)


def range_compress(echoes, filters):
    block_len = filters.shape[-1] // 2
    windows = block_windows(echoes, block_len, 1, 3, echoes.shape[-1] // block_len)
    matrices = complex_matrix(toeplitz_rows(filters, block_len, 3 * block_len))
    product = jnp.einsum(
        "pcanw,caeiw->pceni", windows, matrices, preferred_element_type=jnp.float32
    )
    return product.reshape(echoes.shape)


def azimuth_focus(columns, coeffs):
    block_len = coeffs.shape[-1] // 8
    pulses = columns.shape[-1]
    out_blocks = -(-pulses // block_len)
    windows = block_windows(columns, block_len, 4, 9, out_blocks)
    matrices = complex_matrix(toeplitz_rows(coeffs, block_len, 9 * block_len))
    product = jnp.einsum("sanw,saeiw->seni", windows, matrices, preferred_element_type=jnp.float32)
    return product.reshape(columns.shape[:-1] + (out_blocks * block_len,))[..., :pulses]


def owner_slots(signal, group_starts, group_sizes, offset, slot_width, margin):
    padded = jnp.pad(signal, [(0, 0)] * (signal.ndim - 1) + [(0, margin)])

    def one_group(start_cell, size_cells):
        window_cut = lax.dynamic_slice_in_dim(
            padded, start_cell + offset, slot_width, signal.ndim - 1
        )
        inside = jnp.arange(slot_width, dtype=jnp.int32) + offset < size_cells
        return jnp.where(inside, window_cut, jnp.zeros_like(window_cut))

    return jax.vmap(one_group)(group_starts, group_sizes)


def generic_device(
    raw_echoes, range_taps, beam_weights, channel_order, group_cells, tap_counts, chirp_rates
):
    local_chans = raw_echoes.shape[1]
    all_chans = range_taps.shape[0]
    first_slot = lax.axis_index("chan") * local_chans
    own_channels = lax.dynamic_slice_in_dim(channel_order, first_slot, local_chans)
    selector = (own_channels[:, None] == jnp.arange(all_chans, dtype=jnp.int32)[None, :]).astype(
        jnp.bfloat16
    )
    filters = jnp.dot(
        selector, range_taps.reshape(all_chans, -1), preferred_element_type=jnp.float32
    )
    filters = filters.astype(jnp.bfloat16).reshape(local_chans, 2, -1)
    weights = jnp.dot(
        selector, beam_weights.reshape(all_chans, -1), preferred_element_type=jnp.float32
    )
    weights = weights.reshape(local_chans, 2, -1)
    spectra = range_compress(raw_echoes, filters)
    real_sum = jnp.sum(spectra[:, :, 0] * weights[:, 0] - spectra[:, :, 1] * weights[:, 1], 1)
    imag_sum = jnp.sum(spectra[:, :, 0] * weights[:, 1] + spectra[:, :, 1] * weights[:, 0], 1)
    partial_value = jnp.stack([real_sum, imag_sum], 1)
    tile_count = group_cells.shape[0]
    cell_count = raw_echoes.shape[-1]
    average = cell_count // tile_count
    capacity = average + average // 2
    chan_ways = lax.axis_size("chan")
    half_cap = capacity // chan_ways
    group_starts = jnp.cumsum(group_cells) - group_cells
    chan_offset = lax.axis_index("chan") * half_cap
    summed = lax.psum(partial_value.astype(jnp.bfloat16), "chan")
    outgoing = owner_slots(summed, group_starts, group_cells, chan_offset, half_cap, capacity)
    outgoing = outgoing.transpose(0, 3, 2, 1)
    incoming = lax.all_to_all(outgoing, "tile", split_axis=0, concat_axis=3, tiled=True)
    columns = incoming[0]
    tile_here = lax.axis_index("tile")
    begin_cell = lax.dynamic_index_in_dim(group_starts, tile_here, keepdims=False)
    owned_cells = lax.dynamic_index_in_dim(group_cells, tile_here, keepdims=False)
    local_slot = chan_offset + jnp.arange(half_cap, dtype=jnp.int32)
    inside = local_slot < owned_cells
    count_table = jnp.pad(tap_counts, (0, capacity), mode="edge")
    rate_table = jnp.pad(chirp_rates, (0, capacity), mode="edge")
    count_here = lax.dynamic_slice_in_dim(count_table, begin_cell + chan_offset, half_cap)
    rate_here = lax.dynamic_slice_in_dim(rate_table, begin_cell + chan_offset, half_cap)
    taps_here = chirp_taps(count_here, rate_here, KMAX)
    taps_here = jnp.where(inside[:, None, None], taps_here, jnp.zeros_like(taps_here)).astype(
        jnp.bfloat16
    )
    return azimuth_focus(columns, taps_here)


MESH = pl.DeviceIdType.MESH
BLOCK = 128
STEPS = 5
SPAN = STEPS * BLOCK


def split_bf16(matrix):
    high = matrix.astype(jnp.bfloat16)
    low = (matrix - high.astype(np.float64)).astype(jnp.bfloat16)
    return np.stack([high, low])


def fourier_tables(pulses, local):
    points = 2 * pulses
    freq = np.arange(points)[:, None]
    unit = 2.0 * np.pi / points

    def rotation(index, sign):
        angle = unit * ((freq * index[None, :]) % points)
        return np.cos(angle), sign * np.sin(angle)

    cos_x, sin_x = rotation(np.arange(pulses), -1.0)
    forward = np.stack([np.concatenate([cos_x, sin_x]).T, np.concatenate([-sin_x, cos_x]).T])
    forward = forward.reshape(2, 2, -1, 1, local, 2 * points)
    forward = np.broadcast_to(forward, forward.shape[:3] + (2,) + forward.shape[4:])
    forward = forward.transpose(1, 0, 2, 3, 4, 5).reshape(-1, 2 * points)
    cos_h, sin_h = rotation(pulses - np.arange(points), -1.0)
    taps = np.block([[cos_h, -sin_h], [sin_h, cos_h]])
    cos_y, sin_y = rotation(np.arange(pulses), 1.0)
    inverse = np.block([[cos_y, sin_y], [-sin_y, cos_y]]) / points
    inverse = np.concatenate([inverse[:points], inverse[points:]], 1)
    table = np.concatenate([forward.astype(jnp.bfloat16), *split_bf16(taps)])
    return np.concatenate([table, inverse.astype(jnp.bfloat16)])


def even_series(square, terms):
    value = jnp.full_like(square, terms[-1])
    for term in reversed(terms[:-1]):
        value = value * square + term
    return value


COS_TERMS = [(-1.0) ** n * (2 * np.pi) ** (2 * n) / float(np.prod(np.arange(1, 2 * n + 1, dtype=np.float64))) for n in range(9)]
SIN_TERMS = [(-1.0) ** n * (2 * np.pi) ** (2 * n + 1) / float(np.prod(np.arange(1, 2 * n + 2, dtype=np.float64))) for n in range(9)]


def write_taps(extent, rate, scale, tap_ref, first_tap):
    rows = tap_ref.shape[0] // 2
    length = extent.astype(jnp.int32)
    start = KMAX // 2 - length // 2
    inverse = 1.0 / extent
    turn = 0.5 * rate * extent
    for at in range(0, rows, 32):
        tap = lax.broadcasted_iota(jnp.int32, (32, 2 * BLOCK), 0) + (first_tap + at)
        shifted = tap - start
        inside = (shifted >= 0) & (shifted < length)
        centred = (shifted.astype(jnp.float32) - 0.5 * (extent - 1.0)) * inverse
        square = centred * centred
        envelope = jnp.where(inside, scale * (0.5 + 0.5 * even_series(square, COS_TERMS)), 0.0)
        turns = turn * square
        turns = turns - jnp.floor(turns + 0.5)
        turn_square = turns * turns
        real = envelope * even_series(turn_square, COS_TERMS)
        imag = envelope * (turns * even_series(turn_square, SIN_TERMS))
        tap_ref[at : at + 32] = real.astype(jnp.bfloat16)
        tap_ref[rows + at : rows + at + 32] = imag.astype(jnp.bfloat16)


def focus_kernel(
    half_cap,
    order_hbm,
    cells_hbm,
    raw_ref,
    filter_ref,
    weight_ref,
    count_ref,
    rate_ref,
    table_ref,
    out_ref,
    order_ref,
    cells_ref,
    raw,
    filters,
    weights,
    counts,
    rates,
    table,
    mirror,
    blocks,
    matrices,
    real_sum,
    imag_sum,
    packed,
    columns,
    tap_ref,
    turned,
    first_term,
    load_sems,
    raw_sems,
    send_sem,
    recv_sems,
):
    tiles = packed.shape[0] // 2
    tile_here = lax.axis_index("tile")
    chan_here = lax.axis_index("chan")
    here = 2 * tile_here + chan_here
    local, local_chans, pieces, _ = raw.shape[1:]
    out_blocks = pieces
    pulses = tiles * local
    points = 2 * pulses
    def fetch(source, target, at):
        return pltpu.make_async_copy(source, target, load_sems.at[at])

    def fetch_raw(half):
        return pltpu.make_async_copy(
            raw_ref.at[:, :, pl.ds(half * pieces, pieces)], raw.at[half], raw_sems.at[half]
        )

    get_filters = fetch(filter_ref, filters, 0)
    get_weights = fetch(weight_ref, weights, 1)
    late = [
        fetch(count_ref, counts, 2),
        fetch(rate_ref, rates, 3),
        fetch(table_ref, table, 4),
    ]
    get_order = fetch(order_hbm, order_ref, 5)
    get_cells = fetch(cells_hbm, cells_ref, 6)
    get_order.start()
    get_filters.start()
    fetch_raw(0).start()
    get_weights.start()
    get_cells.start()
    fetch_raw(1).start()
    for copy in late:
        copy.start()

    barrier = pltpu.get_barrier_semaphore()
    everyone = [(tile, chan) for tile in range(tiles) for chan in range(2)]
    for tile, chan in everyone:

        @pl.when(2 * tile + chan != here)
        def _():
            pl.semaphore_signal(
                barrier, inc=1, device_id={"tile": tile, "chan": chan}, device_id_type=MESH
            )

    edge = jnp.zeros((local_chans, 2, 2, local, BLOCK), jnp.bfloat16)
    blocks[:, :, :2] = edge
    blocks[:, :, out_blocks + 2 :] = edge
    row = lax.broadcasted_iota(jnp.int32, (2 * BLOCK, 2 * BLOCK), 0)
    lane = lax.broadcasted_iota(jnp.int32, (2 * BLOCK, 2 * BLOCK), 1)
    mirror[...] = jnp.where(row + lane == 2 * BLOCK - 1, 1.0, 0.0).astype(jnp.bfloat16)
    get_order.wait()
    get_filters.wait()

    physical = [order_ref[chan_here * local_chans + chan] for chan in range(local_chans)]
    own = jnp.concatenate([filters[at].astype(jnp.float32) for at in physical], 0)
    own = own.astype(jnp.bfloat16)
    backward = jnp.concatenate(
        [
            jnp.dot(own[:, 2 * BLOCK :], mirror[...], preferred_element_type=jnp.float32),
            jnp.dot(own[:, : 2 * BLOCK], mirror[...], preferred_element_type=jnp.float32),
            jnp.zeros((2 * local_chans, BLOCK), jnp.float32),
        ],
        1,
    ).astype(jnp.bfloat16)
    def toeplitz(at):
        row = jnp.broadcast_to(backward[at : at + 1], (BLOCK, SPAN))
        return pltpu.roll(row, 1, 1, stride=1, stride_axis=0)

    def write_matrix(chan, part):
        rows = toeplitz(2 * chan + part)
        for step in range(STEPS):
            matrices[chan, step, part] = rows[:, (4 - step) * BLOCK : (5 - step) * BLOCK]

    def spread_rows(half, chan):
        wide = jnp.swapaxes(raw[half, :, chan].astype(jnp.float32), 0, 1).astype(jnp.bfloat16)
        for block in range(pieces // 2):
            at = half * (pieces // 2) + block + 2
            blocks[chan, 0, at] = wide[2 * block]
            blocks[chan, 1, at] = wide[2 * block + 1]

    def compress(chan, first, last):
        total = None
        for step in range(STEPS):
            window = jnp.concatenate(
                [
                    blocks[chan, part, first + step : last + step].reshape(-1, BLOCK)
                    for part in range(2)
                ],
                1,
            )
            real, imag = matrices[chan, step, 0], matrices[chan, step, 1]
            matrix = jnp.concatenate(
                [jnp.concatenate([real, imag], 1), jnp.concatenate([-imag, real], 1)], 0
            )
            term = jnp.dot(window, matrix, preferred_element_type=jnp.float32)
            total = term if total is None else total + term
        return total

    def beamform(chan, first, last, total):
        own_weight = weights[physical[chan]].astype(jnp.float32)
        for block in range(first, last):
            cells = slice(block * BLOCK, (block + 1) * BLOCK)
            weight_real = own_weight[0:1, cells]
            weight_imag = own_weight[1:2, cells]
            real = total[(block - first) * local : (block - first + 1) * local, :BLOCK]
            imag = total[(block - first) * local : (block - first + 1) * local, BLOCK:]
            new_real = weight_real * real - weight_imag * imag
            new_imag = weight_imag * real + weight_real * imag
            if chan > 0:
                new_real += real_sum[block]
                new_imag += imag_sum[block]
            real_sum[block] = new_real
            imag_sum[block] = new_imag

    def phase(group, first, last):
        chans = (2 * group, 2 * group + 1)
        totals = [compress(chan, first, last) for chan in chans]
        for chan, total in zip(chans, totals):
            beamform(chan, first, last, total)

    is_left = lax.broadcasted_iota(jnp.int32, (local, BLOCK), 1) < BLOCK // 2

    def pack(tile, real, imag):
        def put(chan, at):
            cells = slice(at * BLOCK, (at + 1) * BLOCK)
            packed[2 * tile + chan, 0] = real[:, cells].astype(jnp.bfloat16)
            packed[2 * tile + chan, 1] = imag[:, cells].astype(jnp.bfloat16)

        put(0, 0)
        put(1, 2)
        half_real, half_imag = real[:, BLOCK : 2 * BLOCK], imag[:, BLOCK : 2 * BLOCK]
        packed[2 * tile, 2] = jnp.where(
            is_left, half_real, pltpu.roll(half_imag, BLOCK // 2, 1)
        ).astype(jnp.bfloat16)
        packed[2 * tile + 1, 2] = jnp.where(
            is_left, pltpu.roll(half_real, BLOCK // 2, 1), half_imag
        ).astype(jnp.bfloat16)

    half_here, place_here = here // tiles, lax.rem(here, tiles)

    def send(peer):
        return pltpu.make_async_remote_copy(
            src_ref=packed.at[peer],
            dst_ref=columns.at[half_here, :, place_here],
            send_sem=send_sem,
            recv_sem=recv_sems.at[half_here],
            device_id={"tile": peer // 2, "chan": peer % 2},
            device_id_type=MESH,
        )

    def keep(peer):
        return pltpu.make_async_copy(
            packed.at[peer], columns.at[half_here, :, place_here], recv_sems.at[half_here]
        )

    def deliver(tile):
        pair = tile // 2
        parts = range(3 if tile == 0 else 4)
        real = jnp.concatenate([real_sum[4 * pair + at] for at in parts], 1)
        imag = jnp.concatenate([imag_sum[4 * pair + at] for at in parts], 1)
        if tile % 2 == 1:
            both = jnp.concatenate([real, imag], 0)
            both = pltpu.roll(both, 4 * BLOCK - cells_ref[2 * pair], 1)
            real, imag = both[:local], both[local:]
        pack(tile, real, imag)
        if tile == 0:
            pl.semaphore_wait(barrier, 2 * tiles - 1)
        peers = (2 * tile, 2 * tile + 1)
        for peer in peers if tile == 0 else peers[::-1]:

            @pl.when(peer != here)
            def _():
                send(peer).start()

            @pl.when(peer == here)
            def _():
                keep(peer).start()

    groups = local_chans // 2
    for chan in range(2):
        for part in range(2):
            write_matrix(chan, part)
    get_weights.wait()
    fetch_raw(0).wait()
    spread_rows(0, 0)
    write_matrix(2, 0)
    spread_rows(0, 1)
    for group in range(groups):
        first = 2 * group
        more = first + 2 < local_chans
        totals = [compress(first, 0, 3), compress(first + 1, 0, 3)]
        if more:
            write_matrix(first + 2, 1)
            spread_rows(0, first + 2)
            write_matrix(first + 3, 0)
        beamform(first, 0, 3, totals[0])
        if more:
            spread_rows(0, first + 3)
            write_matrix(first + 3, 1)
        beamform(first + 1, 0, 3, totals[1])
        if first + 4 < local_chans:
            write_matrix(first + 4, 0)

    def second_phase():
        fetch_raw(1).wait()
        for chan in range(local_chans):
            spread_rows(1, chan)
        for group in range(groups):
            phase(group, 3, out_blocks)

    get_cells.wait()
    early = tile_here < tiles // 2
    pl.when(early)(second_phase)
    deliver(0)
    pl.when(jnp.logical_not(early))(second_phase)
    for tile in range(1, tiles):
        deliver(tile)
    for copy in late:
        copy.wait()
    begin = 0
    for tile in range(tiles):
        begin += jnp.where(tile < tile_here, cells_ref[tile], 0)
    cell_count = counts.shape[1]

    def own_cells(table):
        wide = jnp.broadcast_to(table.astype(jnp.float32), (8, cell_count))

        def cut(at):
            shift = lax.rem(2 * cell_count - begin - at, cell_count)
            return pltpu.roll(wide, shift, 1)[0:1, :BLOCK]

        return jnp.concatenate([cut(2 * BLOCK * chan_here), cut(BLOCK + BLOCK // 2 * chan_here)], 1)

    extent = own_cells(counts[...])
    place = lax.broadcasted_iota(jnp.int32, (1, 2 * BLOCK), 1)
    place += jnp.where(place < BLOCK, 2 * BLOCK * chan_here, BLOCK // 2 * chan_here)
    live = place < cells_ref[tile_here]
    scale = jnp.where(live, 1.6 / jnp.sqrt(extent), 0.0)
    rate = own_cells(rates[...])
    write_taps(extent, rate, scale, tap_ref, KMAX // 2 - pulses)
    taps = tap_ref[...]
    high = table[2 * points : 4 * points]
    low = table[4 * points : 6 * points]
    response = jnp.dot(high, taps, preferred_element_type=jnp.float32) + jnp.dot(
        low, taps, preferred_element_type=jnp.float32
    )
    turned[...] = response.T

    for half in range(2):
        pltpu.make_async_copy(columns.at[half], columns.at[half], recv_sems.at[half]).wait()
        pieces = [columns[half, at].reshape(BLOCK, BLOCK).T for at in range(3)]
        signal = jnp.concatenate(
            [
                jnp.concatenate(pieces[:2], 1),
                jnp.concatenate([pieces[2][: BLOCK // 2], pieces[2][BLOCK // 2 :]], 1),
            ],
            0,
        )
        term = jnp.dot(
            signal,
            table[2 * half * BLOCK : 2 * (half + 1) * BLOCK],
            preferred_element_type=jnp.float32,
        )
        if half == 0:
            first_term[...] = term
        else:
            image = first_term[...] + term
    slots = image.shape[0]
    real, imag = image[:, :points], image[:, points:]
    tap_real, tap_imag = turned[:slots, :points], turned[:slots, points:]
    product = jnp.concatenate(
        [real * tap_real - imag * tap_imag, real * tap_imag + imag * tap_real], 1
    ).astype(jnp.bfloat16)
    inverse = table[6 * points :]
    result = jnp.dot(
        product[:, :points], inverse[:, :points], preferred_element_type=jnp.float32
    ) + jnp.dot(product[:, points:], inverse[:, points:], preferred_element_type=jnp.float32)
    for part in range(2):
        lanes = slice(part * pulses, (part + 1) * pulses)
        out_ref[pl.ds(BLOCK * chan_here + part, BLOCK, stride=2), :] = result[:BLOCK, lanes]
        out_ref[pl.ds(2 * BLOCK * (1 - chan_here) + part, slots - BLOCK, stride=2), :] = result[
            BLOCK:, lanes
        ]
    sent = packed.at[pl.ds(0, 2 * tiles - 1)]
    pltpu.make_async_copy(sent, sent, send_sem).wait()


def focus_call(raw_echoes, range_taps, beam_weights, order, cells, counts, rates, half_cap):
    local, local_chans, _, cell_count = raw_echoes.shape
    tiles = cells.shape[0]
    pulses = tiles * local
    out_blocks = cell_count // BLOCK
    raw_echoes = raw_echoes.reshape(local, local_chans, 2, out_blocks, BLOCK)
    raw_echoes = raw_echoes.transpose(0, 1, 3, 2, 4).reshape(local, local_chans, -1, BLOCK)
    table = jnp.asarray(fourier_tables(pulses, local))
    counts, rates = counts[None], rates[None]
    arrays = [raw_echoes, range_taps, beam_weights, counts, rates, table]
    total = pltpu.VMEM((out_blocks, local, BLOCK), jnp.float32)
    result = pl.pallas_call(
        functools.partial(focus_kernel, half_cap),
        out_shape=pltpu.VMEM((2 * half_cap, pulses), jnp.float32),
        in_specs=[pl.BlockSpec(memory_space=pl.ANY)] * (2 + len(arrays)),
        out_specs=pl.BlockSpec(memory_space=pltpu.VMEM),
        scratch_shapes=[pltpu.SMEM(order.shape, order.dtype), pltpu.SMEM(cells.shape, cells.dtype)]
        + [pltpu.VMEM((2, local, local_chans, out_blocks, BLOCK), raw_echoes.dtype)]
        + [pltpu.VMEM(array.shape, array.dtype) for array in arrays[1:]]
        + [
            pltpu.VMEM((2 * BLOCK, 2 * BLOCK), jnp.bfloat16),
            pltpu.VMEM((local_chans, 2, out_blocks + 4, local, BLOCK), jnp.bfloat16),
            pltpu.VMEM((local_chans, STEPS, 2, BLOCK, BLOCK), jnp.bfloat16),
            total,
            total,
            pltpu.VMEM((2 * tiles, 3, local, BLOCK), jnp.bfloat16),
            pltpu.VMEM((2, 3, tiles, local, BLOCK), jnp.bfloat16),
            pltpu.VMEM((4 * pulses, 2 * BLOCK), jnp.bfloat16),
            pltpu.VMEM((2 * BLOCK, 4 * pulses), jnp.float32),
            pltpu.VMEM((half_cap, 4 * pulses), jnp.float32),
            pltpu.SemaphoreType.DMA((len(arrays) + 1,)),
            pltpu.SemaphoreType.DMA((2,)),
            pltpu.SemaphoreType.DMA(()),
            pltpu.SemaphoreType.DMA((2,)),
        ],
        compiler_params=pltpu.CompilerParams(
            collective_id=0, has_side_effects=True, vmem_limit_bytes=56 << 20
        ),
    )(order, cells, *arrays)
    return result.reshape(half_cap, 2, pulses)


def on_device(
    raw_echoes, range_taps, beam_weights, channel_order, group_cells, tap_counts, chirp_rates
):
    tiles = group_cells.shape[0]
    local, _, _, cell_count = raw_echoes.shape
    average = cell_count // tiles
    half_cap = (average + average // 2) // lax.axis_size("chan")
    fits = average == 2 * BLOCK and lax.axis_size("chan") == 2 and local == 16 and tiles == 8
    if not fits or range_taps.shape[-1] != 4 * BLOCK:
        return generic_device(
            raw_echoes,
            range_taps,
            beam_weights,
            channel_order,
            group_cells,
            tap_counts,
            chirp_rates,
        )
    return focus_call(
        raw_echoes,
        range_taps,
        beam_weights,
        channel_order,
        group_cells,
        tap_counts,
        chirp_rates,
        half_cap,
    )


def solution(mesh):
    return jax.shard_map(
        on_device,
        mesh=mesh,
        in_specs=(P(("scene", "tile"), "chan", None, None), P(), P(), P(), P(), P(), P()),
        out_specs=P(("scene", "tile", "chan"), None, None),
        check_vma=False,
    )
```
